32 devices in a mesh: groups: 2 (over x), dp: 2 (over core), tensor: 8 (over z, y).
Axes of the slice: x: 2, y: 2, z: 4, core: 2. Of those that a mesh axis runs over, the one named last changes fastest.
Arguments:
- hidden: bfloat16 [4, 1024, 8192], P(('groups', 'dp'), 'tensor'), parts along dimension 0, may hold values from -24 to 24
- query_weight: bfloat16 [8192, 4096], P(None, 'tensor'), may hold values from -0.0625 to 0.0625
- key_weight: bfloat16 [8, 4096, 128], P('tensor'), may hold values from -0.0625 to 0.0625
- value_weight: bfloat16 [8, 4096, 128], P('tensor'), may hold values from -0.0625 to 0.0625
- head_grad: bfloat16 [4, 1024, 4096], P(('groups', 'dp'), None, 'tensor'), parts along dimension 0, may hold values from -6 to 6
- lengths: int32 [4], P(('groups', 'dp')), parts along dimension 0, may hold values from 256 to 1024, as said below
Outputs:
- fisher_key: float32 [16, 4096, 128], P(('groups', 'tensor'), 'dp'), parts along dimension 0
- fisher_value: float32 [16, 4096, 128], P(('groups', 'tensor'), 'dp'), parts along dimension 0
The draws below stay inside these ranges and needn't reach their ends.
There are 2 independent parts, one for each index of `groups`. The reference program is written for one: setup_inputs(seed, part) draws one part's arguments, and reference() takes and returns one part's arrays. A program takes and returns all parts, laid end to end along the dimension named above; an argument that names none is the same for every part. Nothing has to cross between parts.
Inputs may be any that keep to these rules, and one draw needn't show every extreme that they name: `lengths`: some sequence of each part has length 1024.
All inputs are finite; a program needn't handle non-finite values.
Results may differ from the reference program's by a relative error of at most 0.013.
The reference program's roundings to bfloat16 on the way count: a program that leaves them out, or rounds other values in their place, can miss the bound.
Values may be sent and summed in bfloat16 or wider, within the bound.
A program may use at most 256 MiB of HBM per device.

```python
import math
import jax
import jax.numpy as jnp
from jax import lax

D = 8192
HD = 128
QH = 32
KVH = 4
SEQ_LEN = 1024
NSEQ = 2


def draw_hidden(key, part):
    base_key = jax.random.fold_in(jax.random.fold_in(key, 11), 0)
    values = jax.random.normal(base_key, (NSEQ, SEQ_LEN, D), jnp.float32)
    return jnp.clip(values, -24.0, 24.0).astype(jnp.bfloat16)


def draw_lengths(key, part):
    value_key, pick_key = jax.random.split(jax.random.fold_in(key, 23))
    drawn = jax.random.randint(value_key, (NSEQ,), SEQ_LEN // 4, SEQ_LEN + 1)
    chosen = jax.random.randint(pick_key, (), 0, NSEQ)
    return jnp.where(jnp.arange(NSEQ) == chosen, SEQ_LEN, drawn).astype(jnp.int32)


def shard_levels(rng, extent, cuts, least, top_value):
    factor_of, own = 1.0, jax.random.fold_in(rng, 6)
    for dim, shards_of in cuts:
        steps = jnp.exp(jax.random.uniform(jax.random.fold_in(own, dim), (shards_of,), jnp.float32, least / len(cuts), top_value / len(cuts)))
        factor_of = factor_of * jnp.repeat(steps, extent[dim] // shards_of).reshape([-1 if axis == dim else 1 for axis in range(len(extent))])
    return factor_of


def gaussian(own_key, dims, scale, most, shards=(), kind=jnp.bfloat16):
    array = jax.random.normal(own_key, dims, jnp.float32) * scale
    if len(shards) > 0:
        array = shard_levels(own_key, dims, shards, -0.22, 0.18) * array
    return jnp.clip(array, min=-most, max=most).astype(kind)


def setup_inputs(seed: int = 0, part: int = 0) -> dict:
    splits = jax.random.split(jax.random.key(seed), 7)
    own_keys = jax.random.split(jax.random.fold_in(splits[6], part), 7)
    return {
        "hidden": draw_hidden(jax.random.fold_in(jax.random.fold_in(splits[6], part), 71), part),
        "query_weight": gaussian(splits[1], (D, QH * HD), D ** -0.5, 0.0625, ((1, 8),)),
        "key_weight": gaussian(splits[2], (2 * KVH, D // 2, HD), D ** -0.5, 0.0625, ((0, 8),)),
        "value_weight": gaussian(splits[3], (2 * KVH, D // 2, HD), D ** -0.5, 0.0625, ((0, 8),)),
        "head_grad": gaussian(own_keys[4], (NSEQ, SEQ_LEN, QH * HD), 1.0, 6.0, ((0, 2), (2, 8))),
        "lengths": draw_lengths(jax.random.fold_in(jax.random.fold_in(splits[6], part), 71), part),
    }


rope_base = 1000000.0
far_below = -1e+30

def angle_table(length, head_width):
    position = jnp.arange(length, dtype=jnp.float32)[:, None]
    frequency = rope_base ** (-2.0 * jnp.arange(head_width // 2, dtype=jnp.float32) / head_width)
    return (position * frequency)[:, None, :]

def rotate(vectors, angles):
    half_dim = vectors.shape[-1] // 2
    lead_half = vectors[..., :half_dim]
    tail_half = vectors[..., half_dim:]
    cosine = jnp.cos(angles)
    sines = jnp.sin(angles)
    return jnp.concatenate([lead_half * cosine - tail_half * sines, tail_half * cosine + lead_half * sines], axis=-1)

def unrotate(vectors, angles):
    half_dim = vectors.shape[-1] // 2
    lead_half = vectors[..., :half_dim]
    tail_half = vectors[..., half_dim:]
    cosine = jnp.cos(angles)
    sines = jnp.sin(angles)
    return jnp.concatenate([lead_half * cosine + tail_half * sines, tail_half * cosine - lead_half * sines], axis=-1)

def full_rows(weight):
    return weight.reshape(KVH, 2, D // 2, HD).transpose(1, 2, 0, 3).reshape(D, KVH * HD)

def split_rows(matrix):
    return matrix.reshape(2, D // 2, KVH, HD).transpose(2, 0, 1, 3).reshape(2 * KVH, D // 2, HD)

def reference(hidden, query_weight, key_weight, value_weight, head_grad, lengths):
    score_scale = 1.0 / math.sqrt(HD)
    group_size = QH // KVH
    angles = angle_table(SEQ_LEN, HD)
    key_full = full_rows(key_weight)
    value_full = full_rows(value_weight)
    positions = jnp.arange(SEQ_LEN, dtype=jnp.int32)
    causal_ok = positions[:, None] >= positions[None, :]
    fisher_key = jnp.zeros((D, KVH * HD), jnp.float32)
    fisher_value = jnp.zeros((D, KVH * HD), jnp.float32)
    for seq_idx in range(NSEQ):
        seq_rows = hidden[seq_idx]
        queries = rotate(jnp.dot(seq_rows, query_weight, preferred_element_type=jnp.float32).reshape(SEQ_LEN, QH, HD), angles).astype(jnp.bfloat16)
        keys = rotate(jnp.dot(seq_rows, key_full, preferred_element_type=jnp.float32).reshape(SEQ_LEN, KVH, HD), angles).astype(jnp.bfloat16)
        values = jnp.dot(seq_rows, value_full, preferred_element_type=jnp.float32).astype(jnp.bfloat16).reshape(SEQ_LEN, KVH, HD)
        live_rows = (positions < lengths[seq_idx])[:, None]
        upstream = jnp.where(live_rows, head_grad[seq_idx], jnp.zeros_like(head_grad[seq_idx])).reshape(SEQ_LEN, QH, HD)
        query_groups = queries.reshape(SEQ_LEN, KVH, group_size, HD).transpose(1, 2, 0, 3)
        up_groups = upstream.reshape(SEQ_LEN, KVH, group_size, HD).transpose(1, 2, 0, 3)

        def one_group(operands):
            group_queries, group_up, head_keys, head_values = operands
            key_acc = jnp.zeros((SEQ_LEN, HD), jnp.float32)
            value_acc = jnp.zeros((SEQ_LEN, HD), jnp.float32)
            for member in range(group_size):
                query_head = group_queries[member]
                up_head = group_up[member]
                scores = jnp.dot(query_head, head_keys.T, preferred_element_type=jnp.float32) * score_scale
                scores = jnp.where(causal_ok, scores, far_below)
                exp_scores = jnp.exp(scores - lax.optimization_barrier(jnp.max(scores, axis=-1, keepdims=True)))
                prob_rows = exp_scores / lax.optimization_barrier(jnp.sum(exp_scores, axis=-1, keepdims=True))
                dprob = jnp.dot(up_head, head_values.T, preferred_element_type=jnp.float32)
                row_dot = lax.optimization_barrier(jnp.sum(prob_rows * dprob, axis=-1, keepdims=True))
                dscore = (prob_rows * (dprob - row_dot) * score_scale).astype(jnp.bfloat16)
                key_acc = key_acc + jnp.dot(dscore.T, query_head, preferred_element_type=jnp.float32)
                value_acc = value_acc + jnp.dot(prob_rows.astype(jnp.bfloat16).T, up_head, preferred_element_type=jnp.float32)
            return (key_acc, value_acc)
        key_rot, value_acc = lax.map(one_group, (query_groups, up_groups, keys.transpose(1, 0, 2), values.transpose(1, 0, 2)))
        key_gradient = unrotate(key_rot.transpose(1, 0, 2), angles).astype(jnp.bfloat16).reshape(SEQ_LEN, KVH * HD)
        value_grad = value_acc.transpose(1, 0, 2).astype(jnp.bfloat16).reshape(SEQ_LEN, KVH * HD)
        key_sample = jnp.dot(seq_rows.T, key_gradient, preferred_element_type=jnp.float32)
        value_sample = jnp.dot(seq_rows.T, value_grad, preferred_element_type=jnp.float32)
        fisher_key = fisher_key + key_sample * key_sample
        fisher_value = fisher_value + value_sample * value_sample
    return (split_rows(fisher_key), split_rows(fisher_value))
```

```python
import functools
import math

import jax
import jax.numpy as jnp
from jax import lax
from jax.experimental import pallas as pl
from jax.experimental.pallas import tpu as pltpu
from jax.sharding import PartitionSpec as P

MESH = pl.DeviceIdType.MESH

rope_base = 1000000.0
far_below = -1e30


def from_partner(value, axis, stride):
    mask = 2**stride
    pairs = [(source, source ^ mask) for source in range(lax.axis_size(axis))]
    return lax.ppermute(value, axis, pairs)


def angle_table(length, head_width):
    position = jnp.arange(length, dtype=jnp.float32)[:, None]
    frequency = rope_base ** (-2.0 * jnp.arange(head_width // 2, dtype=jnp.float32) / head_width)
    return (position * frequency)[:, None, :]


def rotate(vectors, angles):
    half_dim = vectors.shape[-1] // 2
    lead_half = vectors[..., :half_dim]
    tail_half = vectors[..., half_dim:]
    cosine = jnp.cos(angles)
    sines = jnp.sin(angles)
    return jnp.concatenate(
        [lead_half * cosine - tail_half * sines, tail_half * cosine + lead_half * sines], axis=-1
    )


def unrotate(vectors, angles):
    half_dim = vectors.shape[-1] // 2
    lead_half = vectors[..., :half_dim]
    tail_half = vectors[..., half_dim:]
    cosine = jnp.cos(angles)
    sines = jnp.sin(angles)
    return jnp.concatenate(
        [lead_half * cosine + tail_half * sines, tail_half * cosine - lead_half * sines], axis=-1
    )


def gather_project_kernel(
    count, dp_count, hidden_ref, query_ref, key_ref, value_ref,
    rows_out, own_out, other_out,
    held, weights, partial,
    rows_recv, up_send, down_send, mate_send, load_sem, weight_send, weight_recv,
    share_send, share_recv, partial_send, partial_recv, rows_store, own_store,
):
    me = lax.axis_index("tensor")
    core = lax.axis_index("dp")
    side = lax.rem(me, 2)
    place = lax.div(me, 2)
    mate = me + 1 - 2 * side
    chain = count // 2
    half = held.shape[2]
    query_cols = query_ref.shape[1]
    head_width = key_ref.shape[1]
    own_cols = query_cols + 2 * head_width
    has_up = place < chain - 1
    has_down = place > 0
    share = half // dp_count

    barrier = pltpu.get_barrier_semaphore()
    pl.semaphore_signal(barrier, inc=1, device_id={"tensor": mate}, device_id_type=MESH)
    for step in range(1, dp_count):
        peer = lax.rem(core + step, dp_count)
        pl.semaphore_signal(barrier, inc=1, device_id={"dp": peer}, device_id_type=MESH)

    @pl.when(has_up)
    def _():
        pl.semaphore_signal(barrier, inc=1, device_id={"tensor": me + 2}, device_id_type=MESH)

    @pl.when(has_down)
    def _():
        pl.semaphore_signal(barrier, inc=1, device_id={"tensor": me - 2}, device_id_type=MESH)

    edges = jnp.where(has_up, 1, 0) + jnp.where(has_down, 1, 0)
    pl.semaphore_wait(barrier, dp_count + edges)

    own_half = hidden_ref.at[:, pl.ds(pl.multiple_of(side * half, half), half)]
    mate_half = hidden_ref.at[:, pl.ds(pl.multiple_of((1 - side) * half, half), half)]

    def up_copy(slot, source):
        return pltpu.make_async_remote_copy(
            src_ref=source, dst_ref=held.at[slot], send_sem=up_send.at[slot],
            recv_sem=rows_recv.at[slot], device_id={"tensor": me + 2}, device_id_type=MESH)

    def down_copy(slot, source):
        return pltpu.make_async_remote_copy(
            src_ref=source, dst_ref=held.at[slot], send_sem=down_send.at[slot],
            recv_sem=rows_recv.at[slot], device_id={"tensor": me - 2}, device_id_type=MESH)

    def wait_rows(slot):
        pltpu.make_async_remote_copy(
            src_ref=held.at[slot], dst_ref=held.at[slot], send_sem=mate_send,
            recv_sem=rows_recv.at[slot], device_id={"tensor": mate}, device_id_type=MESH).wait_recv()

    def store_rows(slot):
        return pltpu.make_async_copy(held.at[slot], rows_out.at[slot], rows_store.at[slot])

    def store_own(slot):
        return pltpu.make_async_copy(
            partial.at[slot, :, pl.ds(0, own_cols)], own_out.at[slot], own_store.at[slot])

    def partial_copy(slot):
        return pltpu.make_async_remote_copy(
            src_ref=partial.at[slot, :, pl.ds(query_cols, own_cols)], dst_ref=other_out.at[slot],
            send_sem=partial_send.at[slot], recv_sem=partial_recv.at[slot],
            device_id={"tensor": mate}, device_id_type=MESH)

    to_mate = pltpu.make_async_remote_copy(
        src_ref=mate_half, dst_ref=held.at[me], send_sem=mate_send,
        recv_sem=rows_recv.at[me], device_id={"tensor": mate}, device_id_type=MESH)
    to_mate.start()

    @pl.when(has_up)
    def _():
        up_copy(me, own_half).start()

    @pl.when(has_down)
    def _():
        down_copy(me, own_half).start()

    half_rows = pl.ds(pl.multiple_of(side * half, half), half)
    loads = [
        pltpu.make_async_copy(own_half, held.at[me], load_sem.at[0]),
        pltpu.make_async_copy(
            query_ref.at[half_rows], weights.at[:, pl.ds(0, query_cols)], load_sem.at[1]),
        pltpu.make_async_copy(
            key_ref, weights.at[:, pl.ds(query_cols, head_width)], load_sem.at[2]),
        pltpu.make_async_copy(
            value_ref, weights.at[:, pl.ds(query_cols + head_width, head_width)], load_sem.at[3]),
    ]
    for load in loads:
        load.start()

    share_rows = pl.ds(pl.multiple_of(core * share, share), share)
    mate_cols = pl.ds(own_cols, query_cols)
    weight_copy = pltpu.make_async_remote_copy(
        src_ref=query_ref.at[pl.ds(pl.multiple_of((1 - side) * half + core * share, share), share)],
        dst_ref=weights.at[share_rows, mate_cols], send_sem=weight_send, recv_sem=weight_recv,
        device_id={"tensor": mate}, device_id_type=MESH)

    wait_rows(mate)

    @pl.when(has_up)
    def _():
        up_copy(mate, held.at[mate]).start()

    @pl.when(has_down)
    def _():
        down_copy(mate, held.at[mate]).start()

    weight_copy.start()

    def slot_at(step, which):
        return 2 * step + jnp.where(which == 0, side, 1 - side)

    def receive(distance, which):
        below = place - distance
        above = place + distance

        @pl.when(below >= 0)
        def _():
            slot = slot_at(below, which)
            wait_rows(slot)

            @pl.when(has_up)
            def _():
                up_copy(slot, held.at[slot]).start()

        @pl.when(above < chain)
        def _():
            slot = slot_at(above, which)
            wait_rows(slot)

            @pl.when(has_down)
            def _():
                down_copy(slot, held.at[slot]).start()

    def project(slot):
        store_rows(slot).start()

        @pl.loop(0, weights.shape[1] // 256)
        def _(tile):
            columns = pl.ds(pl.multiple_of(tile * 256, 256), 256)
            partial[slot, :, columns] = jnp.dot(
                held[slot], weights[:, columns], preferred_element_type=jnp.float32)

        partial_copy(slot).start()
        store_own(slot).start()

    def project_at(distance, which):
        below = place - distance
        above = place + distance

        @pl.when(below >= 0)
        def _():
            project(slot_at(below, which))

        @pl.when(above < chain)
        def _():
            project(slot_at(above, which))

    receive(1, 0)
    receive(1, 1)
    for load in loads:
        load.wait()
    weight_copy.wait_recv()
    shares = []
    for step in range(1, dp_count):
        peer = lax.rem(core + step, dp_count)
        shares.append(pltpu.make_async_remote_copy(
            src_ref=weights.at[share_rows, mate_cols], dst_ref=weights.at[share_rows, mate_cols],
            send_sem=share_send.at[step - 1], recv_sem=share_recv.at[step - 1],
            device_id={"dp": peer}, device_id_type=MESH))
    for copy in shares:
        copy.start()
    for copy in shares:
        copy.wait_recv()

    @pl.loop(0, 2)
    def _(which):
        project(slot_at(place, which))

    @pl.loop(0, 2)
    def _(which):
        project_at(1, which)

    @pl.loop(4, 2 * chain)
    def _(step):
        distance = lax.div(step, 2)
        which = lax.rem(step, 2)
        receive(distance, which)
        project_at(distance, which)

    to_mate.wait_send()
    weight_copy.wait_send()
    for copy in shares:
        copy.wait_send()

    @pl.loop(0, count)
    def _(slot):
        partial_copy(slot).wait()
        store_rows(slot).wait()
        store_own(slot).wait()
        origin = lax.div(slot, 2)

        @pl.when(has_up & (origin <= place))
        def _():
            up_copy(slot, held.at[slot]).wait_send()

        @pl.when(has_down & (origin >= place))
        def _():
            down_copy(slot, held.at[slot]).wait_send()


def gather_project(hidden, query_weight, key_weight, value_weight):
    count = lax.axis_size("tensor")
    dp_count = lax.axis_size("dp")
    rows, model_width = hidden.shape
    half = model_width // 2
    query_cols = query_weight.shape[1]
    head_width = key_weight.shape[1]
    own_cols = query_cols + 2 * head_width
    all_cols = own_cols + query_cols
    dma = pltpu.SemaphoreType.DMA
    anywhere = pl.BlockSpec(memory_space=pl.ANY)
    return pl.pallas_call(
        functools.partial(gather_project_kernel, count, dp_count),
        out_shape=(
            jax.ShapeDtypeStruct((count, rows, half), jnp.bfloat16),
            jax.ShapeDtypeStruct((count, rows, own_cols), jnp.float32),
            jax.ShapeDtypeStruct((count, rows, own_cols), jnp.float32),
        ),
        in_specs=[anywhere] * 4,
        out_specs=(anywhere,) * 3,
        scratch_shapes=[
            pltpu.VMEM((count, rows, half), jnp.bfloat16),
            pltpu.VMEM((half, all_cols), jnp.bfloat16),
            pltpu.VMEM((count, rows, all_cols), jnp.float32),
            dma((count,)), dma((count,)), dma((count,)), dma, dma((4,)), dma, dma,
            dma((dp_count - 1,)), dma((dp_count - 1,)), dma((count,)), dma((count,)),
            dma((count,)), dma((count,)),
        ],
        compiler_params=pltpu.CompilerParams(
            collective_id=0, has_side_effects=True, vmem_limit_bytes=52 * 2**20),
    )(hidden, query_weight, key_weight, value_weight)


def local(hidden, query_weight, key_weight, value_weight, head_grad, lengths):
    seq_count, tok_rows, model_width = hidden.shape
    length = tok_rows * lax.axis_size("tensor")
    half_width = model_width // 2
    head_width = key_weight.shape[2]
    heads_here = query_weight.shape[1] // head_width
    query_cols = heads_here * head_width
    score_scale = 1.0 / math.sqrt(head_width)
    angles = angle_table(length, head_width)
    half_rows, own_part, other_part = gather_project(
        hidden[0], query_weight, key_weight[0], value_weight[0]
    )
    half_rows = half_rows.reshape(seq_count, length, half_width)
    own_part = own_part.reshape(seq_count, length, -1)
    other_part = other_part.reshape(seq_count, length, -1)
    query_sum = own_part[..., :query_cols] + other_part[..., 2 * head_width :]
    kv_mixed = own_part[..., query_cols:] + other_part[..., : 2 * head_width]
    queries = rotate(
        query_sum.reshape(seq_count, length, heads_here, head_width), angles
    ).astype(jnp.bfloat16)
    keys = rotate(kv_mixed[..., :head_width][:, :, None, :], angles)[:, :, 0, :].astype(
        jnp.bfloat16
    )
    values = kv_mixed[..., head_width:].astype(jnp.bfloat16)
    live_rows = jnp.arange(length, dtype=jnp.int32)[None, :] < lengths[:, None]
    upstream = jnp.where(live_rows[:, :, None], head_grad, jnp.zeros_like(head_grad)).reshape(
        seq_count, length, heads_here, head_width
    )
    block_rows = 512
    block_count = length // block_rows
    kv_accum = jnp.zeros((seq_count, length, 2 * head_width), jnp.float32)
    for block_idx in range(block_count):
        row_begin = block_idx * block_rows
        row_end = row_begin + block_rows
        query_block = queries[:, row_begin:row_end]
        up_block = upstream[:, row_begin:row_end]
        key_tile_block = keys[:, :row_end]
        value_block = values[:, :row_end]
        scores = (
            jnp.einsum(
                "sqhd,skd->shqk", query_block, key_tile_block, preferred_element_type=jnp.float32
            )
            * score_scale
        )
        causal_ok = (row_begin + jnp.arange(block_rows))[:, None] >= jnp.arange(row_end)[None, :]
        scores = jnp.where(causal_ok, scores, far_below)
        exp_scores = jnp.exp(scores - jnp.max(scores, axis=-1, keepdims=True))
        prob_rows = exp_scores / jnp.sum(exp_scores, axis=-1, keepdims=True)
        dprob = jnp.einsum(
            "sqhd,skd->shqk", up_block, value_block, preferred_element_type=jnp.float32
        )
        row_dot = jnp.sum(prob_rows * dprob, axis=-1, keepdims=True)
        dscore = (prob_rows * (dprob - row_dot) * score_scale).astype(jnp.bfloat16)
        key_portion = jnp.einsum(
            "shqk,sqhd->skd", dscore, query_block, preferred_element_type=jnp.float32
        )
        value_part = jnp.einsum(
            "shqk,sqhd->skd",
            prob_rows.astype(jnp.bfloat16),
            up_block,
            preferred_element_type=jnp.float32,
        )
        block_grad = jnp.concatenate([key_portion, value_part], axis=-1)
        kv_accum = kv_accum + jnp.pad(block_grad, ((0, 0), (0, length - row_end), (0, 0)))
    kv_accum = kv_accum + from_partner(kv_accum, "tensor", 0)
    key_gradient = unrotate(kv_accum[..., :head_width][:, :, None, :], angles)[:, :, 0, :]
    key_value_gradient = jnp.concatenate(
        [key_gradient, kv_accum[..., head_width:]], axis=-1
    ).astype(jnp.bfloat16)
    sample_count = jnp.einsum(
        "jyv,jyo->jvo", half_rows, key_value_gradient, preferred_element_type=jnp.float32
    )
    squares = jnp.sum(sample_count * sample_count, axis=0)
    fisher_key, fisher_value = (
        lax.psum_scatter(squares[:, :head_width], "dp", scatter_dimension=0, tiled=True),
        lax.psum_scatter(squares[:, head_width:], "dp", scatter_dimension=0, tiled=True),
    )
    return (fisher_key[None], fisher_value[None])


def solution(mesh):
    in_specs = (
        P(("groups", "dp"), "tensor", None),
        P(None, "tensor"),
        P("tensor", None, None),
        P("tensor", None, None),
        P(("groups", "dp"), None, "tensor"),
        P(("groups", "dp")),
    )
    out_specs = (P(("groups", "tensor"), "dp", None), P(("groups", "tensor"), "dp", None))
    return jax.shard_map(local, mesh=mesh, in_specs=in_specs, out_specs=out_specs, check_vma=False)
```

```python
import functools
import math

import jax
import jax.numpy as jnp
from jax import lax
from jax.experimental import pallas as pl
from jax.experimental.pallas import tpu as pltpu
from jax.sharding import PartitionSpec as P

MESH = pl.DeviceIdType.MESH

rope_base = 1000000.0
far_below = -1e30


def angle_table(length, head_width):
    position = jnp.arange(length, dtype=jnp.float32)[:, None]
    frequency = rope_base ** (-2.0 * jnp.arange(head_width // 2, dtype=jnp.float32) / head_width)
    return position * frequency


def gather_project_kernel(
    count, dp_count, hidden_ref, query_ref, key_ref, value_ref,
    rows_out, own_out, other_out,
    held, weights, partial,
    rows_recv, up_send, down_send, mate_send, load_sem, weight_send, weight_recv,
    share_send, share_recv, partial_send, partial_recv, rows_store, own_store,
):
    me = lax.axis_index("tensor")
    core = lax.axis_index("dp")
    side = lax.rem(me, 2)
    place = lax.div(me, 2)
    mate = me + 1 - 2 * side
    chain = count // 2
    half = held.shape[2]
    query_cols = query_ref.shape[1]
    head_width = key_ref.shape[1]
    own_cols = query_cols + 2 * head_width
    has_up = place < chain - 1
    has_down = place > 0
    share = half // dp_count

    barrier = pltpu.get_barrier_semaphore()
    pl.semaphore_signal(barrier, inc=1, device_id={"tensor": mate}, device_id_type=MESH)
    for step in range(1, dp_count):
        peer = lax.rem(core + step, dp_count)
        pl.semaphore_signal(barrier, inc=1, device_id={"dp": peer}, device_id_type=MESH)

    @pl.when(has_up)
    def _():
        pl.semaphore_signal(barrier, inc=1, device_id={"tensor": me + 2}, device_id_type=MESH)

    @pl.when(has_down)
    def _():
        pl.semaphore_signal(barrier, inc=1, device_id={"tensor": me - 2}, device_id_type=MESH)

    edges = jnp.where(has_up, 1, 0) + jnp.where(has_down, 1, 0)
    pl.semaphore_wait(barrier, dp_count + edges)

    own_half = hidden_ref.at[:, pl.ds(pl.multiple_of(side * half, half), half)]
    mate_half = hidden_ref.at[:, pl.ds(pl.multiple_of((1 - side) * half, half), half)]

    def up_copy(slot, source):
        return pltpu.make_async_remote_copy(
            src_ref=source, dst_ref=held.at[slot], send_sem=up_send.at[slot],
            recv_sem=rows_recv.at[slot], device_id={"tensor": me + 2}, device_id_type=MESH)

    def down_copy(slot, source):
        return pltpu.make_async_remote_copy(
            src_ref=source, dst_ref=held.at[slot], send_sem=down_send.at[slot],
            recv_sem=rows_recv.at[slot], device_id={"tensor": me - 2}, device_id_type=MESH)

    def wait_rows(slot):
        pltpu.make_async_remote_copy(
            src_ref=held.at[slot], dst_ref=held.at[slot], send_sem=mate_send,
            recv_sem=rows_recv.at[slot], device_id={"tensor": mate}, device_id_type=MESH).wait_recv()

    def store_rows(slot):
        return pltpu.make_async_copy(held.at[slot], rows_out.at[slot], rows_store.at[slot])

    def store_own(slot):
        return pltpu.make_async_copy(
            partial.at[slot, :, pl.ds(0, own_cols)], own_out.at[slot], own_store.at[slot])

    def partial_copy(slot):
        return pltpu.make_async_remote_copy(
            src_ref=partial.at[slot, :, pl.ds(query_cols, own_cols)], dst_ref=other_out.at[slot],
            send_sem=partial_send.at[slot], recv_sem=partial_recv.at[slot],
            device_id={"tensor": mate}, device_id_type=MESH)

    to_mate = pltpu.make_async_remote_copy(
        src_ref=mate_half, dst_ref=held.at[me], send_sem=mate_send,
        recv_sem=rows_recv.at[me], device_id={"tensor": mate}, device_id_type=MESH)
    to_mate.start()

    @pl.when(has_up)
    def _():
        up_copy(me, own_half).start()

    @pl.when(has_down)
    def _():
        down_copy(me, own_half).start()

    half_rows = pl.ds(pl.multiple_of(side * half, half), half)
    loads = [
        pltpu.make_async_copy(own_half, held.at[me], load_sem.at[0]),
        pltpu.make_async_copy(
            query_ref.at[half_rows], weights.at[:, pl.ds(0, query_cols)], load_sem.at[1]),
        pltpu.make_async_copy(
            key_ref, weights.at[:, pl.ds(query_cols, head_width)], load_sem.at[2]),
        pltpu.make_async_copy(
            value_ref, weights.at[:, pl.ds(query_cols + head_width, head_width)], load_sem.at[3]),
    ]
    for load in loads:
        load.start()

    share_rows = pl.ds(pl.multiple_of(core * share, share), share)
    mate_cols = pl.ds(own_cols, query_cols)
    weight_copy = pltpu.make_async_remote_copy(
        src_ref=query_ref.at[pl.ds(pl.multiple_of((1 - side) * half + core * share, share), share)],
        dst_ref=weights.at[share_rows, mate_cols], send_sem=weight_send, recv_sem=weight_recv,
        device_id={"tensor": mate}, device_id_type=MESH)

    wait_rows(mate)

    @pl.when(has_up)
    def _():
        up_copy(mate, held.at[mate]).start()

    @pl.when(has_down)
    def _():
        down_copy(mate, held.at[mate]).start()

    weight_copy.start()

    def slot_at(step, which):
        return 2 * step + jnp.where(which == 0, side, 1 - side)

    def receive(distance, which):
        below = place - distance
        above = place + distance

        @pl.when(below >= 0)
        def _():
            slot = slot_at(below, which)
            wait_rows(slot)

            @pl.when(has_up)
            def _():
                up_copy(slot, held.at[slot]).start()

        @pl.when(above < chain)
        def _():
            slot = slot_at(above, which)
            wait_rows(slot)

            @pl.when(has_down)
            def _():
                down_copy(slot, held.at[slot]).start()

    def project(slot):
        store_rows(slot).start()

        @pl.loop(0, weights.shape[1] // 256)
        def _(tile):
            columns = pl.ds(pl.multiple_of(tile * 256, 256), 256)
            partial[slot, :, columns] = jnp.dot(
                held[slot], weights[:, columns], preferred_element_type=jnp.float32)

        partial_copy(slot).start()
        store_own(slot).start()

    def project_at(distance, which):
        below = place - distance
        above = place + distance

        @pl.when(below >= 0)
        def _():
            project(slot_at(below, which))

        @pl.when(above < chain)
        def _():
            project(slot_at(above, which))

    receive(1, 0)
    receive(1, 1)
    for load in loads:
        load.wait()
    weight_copy.wait_recv()
    shares = []
    for step in range(1, dp_count):
        peer = lax.rem(core + step, dp_count)
        shares.append(pltpu.make_async_remote_copy(
            src_ref=weights.at[share_rows, mate_cols], dst_ref=weights.at[share_rows, mate_cols],
            send_sem=share_send.at[step - 1], recv_sem=share_recv.at[step - 1],
            device_id={"dp": peer}, device_id_type=MESH))
    for copy in shares:
        copy.start()
    for copy in shares:
        copy.wait_recv()

    @pl.loop(0, 2)
    def _(which):
        project(slot_at(place, which))

    @pl.loop(0, 2)
    def _(which):
        project_at(1, which)

    @pl.loop(4, 2 * chain)
    def _(step):
        distance = lax.div(step, 2)
        which = lax.rem(step, 2)
        receive(distance, which)
        project_at(distance, which)

    to_mate.wait_send()
    weight_copy.wait_send()
    for copy in shares:
        copy.wait_send()

    @pl.loop(0, count)
    def _(slot):
        partial_copy(slot).wait()
        store_rows(slot).wait()
        store_own(slot).wait()
        origin = lax.div(slot, 2)

        @pl.when(has_up & (origin <= place))
        def _():
            up_copy(slot, held.at[slot]).wait_send()

        @pl.when(has_down & (origin >= place))
        def _():
            down_copy(slot, held.at[slot]).wait_send()


def gather_project(hidden, query_weight, key_weight, value_weight):
    count = lax.axis_size("tensor")
    dp_count = lax.axis_size("dp")
    rows, model_width = hidden.shape
    half = model_width // 2
    query_cols = query_weight.shape[1]
    head_width = key_weight.shape[1]
    own_cols = query_cols + 2 * head_width
    all_cols = own_cols + query_cols
    dma = pltpu.SemaphoreType.DMA
    anywhere = pl.BlockSpec(memory_space=pl.ANY)
    return pl.pallas_call(
        functools.partial(gather_project_kernel, count, dp_count),
        out_shape=(
            jax.ShapeDtypeStruct((count, rows, half), jnp.bfloat16),
            jax.ShapeDtypeStruct((count, rows, own_cols), jnp.float32),
            jax.ShapeDtypeStruct((count, rows, own_cols), jnp.float32),
        ),
        in_specs=[anywhere] * 4,
        out_specs=(anywhere,) * 3,
        scratch_shapes=[
            pltpu.VMEM((count, rows, half), jnp.bfloat16),
            pltpu.VMEM((half, all_cols), jnp.bfloat16),
            pltpu.VMEM((count, rows, all_cols), jnp.float32),
            dma((count,)), dma((count,)), dma((count,)), dma, dma((4,)), dma, dma,
            dma((dp_count - 1,)), dma((dp_count - 1,)), dma((count,)), dma((count,)),
            dma((count,)), dma((count,)),
        ],
        compiler_params=pltpu.CompilerParams(
            collective_id=0, has_side_effects=True, vmem_limit_bytes=52 * 2**20),
    )(hidden, query_weight, key_weight, value_weight)

def swap_halves(vectors):
    return pltpu.roll(vectors, vectors.shape[-1] // 2, axis=1)


def attend_kernel(
    dp_count, head_width, lengths_ref, own_ref, other_ref, up_ref, cosine_ref, sine_ref, rows_ref,
    squares_out, peer_out,
    queries, keys, values, upstream, rows, grads, mate_grads, rounded, peer_squares,
    rows_load, grad_send, grad_recv, peer_send, peer_recv,
):
    me = lax.axis_index("tensor")
    core = lax.axis_index("dp")
    mate = me + 1 - 2 * lax.rem(me, 2)
    blocks, stacked, _ = queries.shape
    heads = stacked // head_width
    step_rows = head_width
    query_cols = heads * head_width
    scale = 1.0 / math.sqrt(head_width)
    share = squares_out.shape[0]
    tile = 256
    tiles = share // tile

    barrier = pltpu.get_barrier_semaphore()
    pl.semaphore_signal(barrier, inc=1, device_id={"tensor": mate}, device_id_type=MESH)
    for step in range(1, dp_count):
        peer = lax.rem(core + step, dp_count)
        pl.semaphore_signal(barrier, inc=1, device_id={"dp": peer}, device_id_type=MESH)

    load = pltpu.make_async_copy(rows_ref, rows, rows_load)
    load.start()
    live = lengths_ref[0]

    @pl.loop(0, blocks)
    def _(block):
        here = pl.ds(pl.multiple_of(block * step_rows, step_rows), step_rows)
        cosine = cosine_ref[here, :]
        sine = sine_ref[here, :]
        position = block * step_rows + lax.broadcasted_iota(jnp.int32, (step_rows, head_width), 0)
        alive = position < live
        for head in range(heads):
            columns = slice(head * head_width, (head + 1) * head_width)
            shifted = slice((head + 2) * head_width, (head + 3) * head_width)
            mixed = own_ref[here, columns] + other_ref[here, shifted]
            turned = mixed * cosine + swap_halves(mixed) * sine
            queries[block, columns, :] = turned.astype(jnp.bfloat16)
            gradient = up_ref[here, columns].astype(jnp.float32)
            upstream[block, columns, :] = jnp.where(alive, gradient, 0.0).astype(jnp.bfloat16)
        mixed = own_ref[here, query_cols:query_cols + head_width] + other_ref[here, :head_width]
        keys[here, :] = (mixed * cosine + swap_halves(mixed) * sine).astype(jnp.bfloat16)
        values[here, :] = (
            own_ref[here, query_cols + head_width:] + other_ref[here, head_width:2 * head_width]
        ).astype(jnp.bfloat16)

    pl.semaphore_wait(barrier, dp_count)

    def grad_copy(block):
        return pltpu.make_async_remote_copy(
            src_ref=grads.at[block], dst_ref=mate_grads.at[block],
            send_sem=grad_send.at[block], recv_sem=grad_recv.at[block],
            device_id={"tensor": mate}, device_id_type=MESH)

    wide = 2 * head_width
    contract_last = (((1,), (1,)), ((), ()))
    for block in reversed(range(blocks)):
        extent = (block + 1) * step_rows
        for chunk in range(stacked // wide):
            chunk_rows = slice(chunk * wide, (chunk + 1) * wide)
            query = queries[block, chunk_rows, :]
            above = upstream[block, chunk_rows, :]
            scores = lax.dot_general(
                keys[:extent, :], query, contract_last, preferred_element_type=jnp.float32)
            key_at = lax.broadcasted_iota(jnp.int32, (step_rows, wide), 0)
            query_at = lax.rem(lax.broadcasted_iota(jnp.int32, (step_rows, wide), 1), step_rows)
            corner = jnp.where(key_at <= query_at, scores[extent - step_rows:], far_below)
            if block > 0:
                scores = jnp.concatenate([scores[:extent - step_rows], corner], axis=0)
            else:
                scores = corner
            peak = jnp.max(scores, axis=0, keepdims=True)
            powers = jnp.exp((scores - peak) * scale)
            prob = powers * (1.0 / jnp.sum(powers, axis=0, keepdims=True))
            dprob = lax.dot_general(
                values[:extent, :], above, contract_last, preferred_element_type=jnp.float32)
            row_dot = jnp.sum(prob * dprob, axis=0, keepdims=True)
            dscore = (prob * (dprob - row_dot) * scale).astype(jnp.bfloat16)
            key_part = jnp.dot(dscore, query, preferred_element_type=jnp.float32)
            value_part = jnp.dot(
                prob.astype(jnp.bfloat16), above, preferred_element_type=jnp.float32)
            key_part = key_part.reshape(block + 1, step_rows, head_width)
            value_part = value_part.reshape(block + 1, step_rows, head_width)
            if block == blocks - 1 and chunk == 0:
                grads[:, :, :head_width] = key_part
                grads[:, :, head_width:] = value_part
            else:
                grads[:block + 1, :, :head_width] += key_part
                grads[:block + 1, :, head_width:] += value_part
        grad_copy(block).start()

    for block in reversed(range(blocks)):
        here = slice(block * step_rows, (block + 1) * step_rows)
        grad_copy(block).wait_recv()
        key_grad = grads[block, :, :head_width] + mate_grads[block, :, :head_width]
        key_grad = key_grad * cosine_ref[here, :] - swap_halves(key_grad) * sine_ref[here, :]
        rounded[here, :head_width] = key_grad.astype(jnp.bfloat16)
        rounded[here, head_width:] = (
            grads[block, :, head_width:] + mate_grads[block, :, head_width:]
        ).astype(jnp.bfloat16)
    load.wait()

    def squares_of(start):
        columns = pl.ds(pl.multiple_of(start, tile), tile)
        sample = lax.dot_general(
            rows[:, columns], rounded[...], (((0,), (0,)), ((), ())),
            preferred_element_type=jnp.float32)
        return sample * sample

    def peer_copy(step, index):
        here = pl.ds(pl.multiple_of(index * tile, tile), tile)
        return pltpu.make_async_remote_copy(
            src_ref=peer_squares.at[step - 1, here], dst_ref=peer_out.at[step - 1, here],
            send_sem=peer_send.at[step - 1, index], recv_sem=peer_recv.at[step - 1, index],
            device_id={"dp": lax.rem(core + step, dp_count)}, device_id_type=MESH)

    for step in range(1, dp_count):
        @pl.loop(0, tiles)
        def _(index):
            here = pl.ds(pl.multiple_of(index * tile, tile), tile)
            start = lax.rem(core + step, dp_count) * share + index * tile
            peer_squares[step - 1, here, :] = squares_of(start)
            peer_copy(step, index).start()

    @pl.loop(0, tiles)
    def _(index):
        here = pl.ds(pl.multiple_of(index * tile, tile), tile)
        squares_out[here, :] = squares_of(core * share + index * tile)

    for block in range(blocks):
        grad_copy(block).wait_send()
    for step in range(1, dp_count):
        @pl.loop(0, tiles)
        def _(index):
            peer_copy(step, index).wait()


def attend(lengths, own_part, other_part, head_grad, cosine, sine, half_rows, head_width):
    dp_count = lax.axis_size("dp")
    length, half = half_rows.shape
    heads = head_grad.shape[1] // head_width
    blocks = length // head_width
    share = half // dp_count
    wide = 2 * head_width
    dma = pltpu.SemaphoreType.DMA
    here = pl.BlockSpec(memory_space=pltpu.VMEM)
    anywhere = pl.BlockSpec(memory_space=pl.ANY)
    return pl.pallas_call(
        functools.partial(attend_kernel, dp_count, head_width),
        out_shape=(
            jax.ShapeDtypeStruct((share, wide), jnp.float32),
            jax.ShapeDtypeStruct((dp_count - 1, share, wide), jnp.float32),
        ),
        in_specs=[pl.BlockSpec(memory_space=pltpu.SMEM)] + [here] * 5 + [anywhere],
        out_specs=(here, anywhere),
        scratch_shapes=[
            pltpu.VMEM((blocks, heads * head_width, head_width), jnp.bfloat16),
            pltpu.VMEM((length, head_width), jnp.bfloat16),
            pltpu.VMEM((length, head_width), jnp.bfloat16),
            pltpu.VMEM((blocks, heads * head_width, head_width), jnp.bfloat16),
            pltpu.VMEM((length, half), jnp.bfloat16),
            pltpu.VMEM((blocks, head_width, wide), jnp.float32),
            pltpu.VMEM((blocks, head_width, wide), jnp.float32),
            pltpu.VMEM((length, wide), jnp.bfloat16),
            pltpu.VMEM((dp_count - 1, share, wide), jnp.float32),
            dma, dma((blocks,)), dma((blocks,)),
            dma((dp_count - 1, share // 256)), dma((dp_count - 1, share // 256)),
        ],
        compiler_params=pltpu.CompilerParams(
            collective_id=1, has_side_effects=True, vmem_limit_bytes=56 * 2**20),
    )(lengths, own_part, other_part, head_grad, cosine, sine, half_rows)


def local(hidden, query_weight, key_weight, value_weight, head_grad, lengths):
    head_width = key_weight.shape[2]
    length = head_grad.shape[1]
    angles = angle_table(length, head_width)
    cosine = jnp.cos(angles)
    sine = jnp.sin(angles)
    cosine = jnp.concatenate([cosine, cosine], axis=-1)
    sine = jnp.concatenate([-sine, sine], axis=-1)
    half_rows, own_part, other_part = gather_project(
        hidden[0], query_weight, key_weight[0], value_weight[0]
    )
    own_squares, peer_squares = attend(
        lengths, own_part.reshape(length, -1), other_part.reshape(length, -1), head_grad[0],
        cosine, sine, half_rows.reshape(length, -1), head_width,
    )
    squares = own_squares + jnp.sum(peer_squares, axis=0)
    return (squares[None, :, :head_width], squares[None, :, head_width:])


def solution(mesh):
    in_specs = (
        P(("groups", "dp"), "tensor", None),
        P(None, "tensor"),
        P("tensor", None, None),
        P("tensor", None, None),
        P(("groups", "dp"), None, "tensor"),
        P(("groups", "dp")),
    )
    out_specs = (P(("groups", "tensor"), "dp", None), P(("groups", "tensor"), "dp", None))
    return jax.shard_map(local, mesh=mesh, in_specs=in_specs, out_specs=out_specs, check_vma=False)
```

```python
import functools
import math

import jax
import jax.numpy as jnp
import numpy as np
from jax import lax
from jax.experimental import pallas as pl
from jax.experimental.pallas import tpu as pltpu
from jax.sharding import PartitionSpec as P

MESH = pl.DeviceIdType.MESH

rope_base = 1000000.0
far_below = -1e30


def turn_table(length, head_width):
    position = np.arange(length, dtype=np.float64)[:, None]
    frequency = rope_base ** (-2.0 * np.arange(head_width // 2, dtype=np.float64) / head_width)
    angles = position * frequency
    return np.concatenate([np.cos(angles), np.sin(angles)], axis=-1).astype(np.float32)


def swap_halves(vectors):
    return pltpu.roll(vectors, vectors.shape[-1] // 2, axis=1)


def cosine_sine(table):
    other = swap_halves(table)
    lead = lax.broadcasted_iota(jnp.int32, table.shape, 1) < table.shape[1] // 2
    return jnp.where(lead, table, other), jnp.where(lead, -other, table)


def gather_project_kernel(
    count, dp_count, lengths_ref, gradient_ref, table_ref,
    hidden_ref, query_ref, key_ref, value_ref,
    rows_out, queries_out, pairs_out, upstream_out,
    held, weights, partial, other, queries, pairs, upstream,
    rows_recv, up_send, down_send, mate_send, load_sem, weight_send, weight_recv,
    share_send, share_recv, partial_send, partial_recv, rows_store, queries_store, pairs_store,
    upstream_store,
):
    me = lax.axis_index("tensor")
    core = lax.axis_index("dp")
    side = lax.rem(me, 2)
    place = lax.div(me, 2)
    mate = me + 1 - 2 * side
    chain = count // 2
    half = held.shape[2]
    query_cols = query_ref.shape[1]
    head_width = key_ref.shape[1]
    own_cols = query_cols + 2 * head_width
    has_up = place < chain - 1
    has_down = place > 0
    share = half // dp_count

    barrier = pltpu.get_barrier_semaphore()
    pl.semaphore_signal(barrier, inc=1, device_id={"tensor": mate}, device_id_type=MESH)
    for step in range(1, dp_count):
        peer = lax.rem(core + step, dp_count)
        pl.semaphore_signal(barrier, inc=1, device_id={"dp": peer}, device_id_type=MESH)

    @pl.when(has_up)
    def _():
        pl.semaphore_signal(barrier, inc=1, device_id={"tensor": me + 2}, device_id_type=MESH)

    @pl.when(has_down)
    def _():
        pl.semaphore_signal(barrier, inc=1, device_id={"tensor": me - 2}, device_id_type=MESH)

    edges = jnp.where(has_up, 1, 0) + jnp.where(has_down, 1, 0)
    pl.semaphore_wait(barrier, dp_count + edges)

    own_half = hidden_ref.at[:, pl.ds(pl.multiple_of(side * half, half), half)]
    mate_half = hidden_ref.at[:, pl.ds(pl.multiple_of((1 - side) * half, half), half)]

    def up_copy(slot, source):
        return pltpu.make_async_remote_copy(
            src_ref=source, dst_ref=held.at[slot], send_sem=up_send.at[slot],
            recv_sem=rows_recv.at[slot], device_id={"tensor": me + 2}, device_id_type=MESH)

    def down_copy(slot, source):
        return pltpu.make_async_remote_copy(
            src_ref=source, dst_ref=held.at[slot], send_sem=down_send.at[slot],
            recv_sem=rows_recv.at[slot], device_id={"tensor": me - 2}, device_id_type=MESH)

    def wait_rows(slot):
        pltpu.make_async_remote_copy(
            src_ref=held.at[slot], dst_ref=held.at[slot], send_sem=mate_send,
            recv_sem=rows_recv.at[slot], device_id={"tensor": mate}, device_id_type=MESH).wait_recv()

    def store_rows(slot):
        return pltpu.make_async_copy(held.at[slot], rows_out.at[slot], rows_store.at[slot])

    def store_queries(slot):
        return pltpu.make_async_copy(queries.at[slot], queries_out.at[slot], queries_store.at[slot])

    def store_pairs(slot):
        return pltpu.make_async_copy(pairs.at[slot], pairs_out.at[slot], pairs_store.at[slot])

    def partial_copy(slot):
        return pltpu.make_async_remote_copy(
            src_ref=partial.at[slot, :, pl.ds(query_cols, own_cols)], dst_ref=other.at[slot],
            send_sem=partial_send.at[slot], recv_sem=partial_recv.at[slot],
            device_id={"tensor": mate}, device_id_type=MESH)

    to_mate = pltpu.make_async_remote_copy(
        src_ref=mate_half, dst_ref=held.at[me], send_sem=mate_send,
        recv_sem=rows_recv.at[me], device_id={"tensor": mate}, device_id_type=MESH)
    to_mate.start()

    @pl.when(has_up)
    def _():
        up_copy(me, own_half).start()

    @pl.when(has_down)
    def _():
        down_copy(me, own_half).start()

    half_rows = pl.ds(pl.multiple_of(side * half, half), half)
    loads = [
        pltpu.make_async_copy(own_half, held.at[me], load_sem.at[0]),
        pltpu.make_async_copy(
            query_ref.at[half_rows], weights.at[:, pl.ds(0, query_cols)], load_sem.at[1]),
        pltpu.make_async_copy(
            key_ref, weights.at[:, pl.ds(query_cols, head_width)], load_sem.at[2]),
        pltpu.make_async_copy(
            value_ref, weights.at[:, pl.ds(query_cols + head_width, head_width)], load_sem.at[3]),
    ]
    for load in loads:
        load.start()

    share_rows = pl.ds(pl.multiple_of(core * share, share), share)
    mate_cols = pl.ds(own_cols, query_cols)
    weight_copy = pltpu.make_async_remote_copy(
        src_ref=query_ref.at[pl.ds(pl.multiple_of((1 - side) * half + core * share, share), share)],
        dst_ref=weights.at[share_rows, mate_cols], send_sem=weight_send, recv_sem=weight_recv,
        device_id={"tensor": mate}, device_id_type=MESH)

    live = lengths_ref[0]
    rows = held.shape[1]
    heads = query_cols // head_width

    @pl.loop(0, count)
    def _(slot):
        here = pl.ds(pl.multiple_of(slot * rows, rows), rows)
        position = slot * rows + lax.broadcasted_iota(jnp.int32, (rows, head_width), 0)
        for head in range(heads):
            gradient = gradient_ref[here, head * head_width:(head + 1) * head_width]
            upstream[slot, head * rows:(head + 1) * rows, :] = jnp.where(
                position < live, gradient.astype(jnp.float32), 0.0).astype(jnp.bfloat16)

    store_upstream = pltpu.make_async_copy(upstream, upstream_out, upstream_store)
    store_upstream.start()
    wait_rows(mate)

    @pl.when(has_up)
    def _():
        up_copy(mate, held.at[mate]).start()

    @pl.when(has_down)
    def _():
        down_copy(mate, held.at[mate]).start()

    weight_copy.start()

    def slot_at(step, which):
        return 2 * step + jnp.where(which == 0, side, 1 - side)

    def receive(distance, which):
        below = place - distance
        above = place + distance

        @pl.when(below >= 0)
        def _():
            slot = slot_at(below, which)
            wait_rows(slot)

            @pl.when(has_up)
            def _():
                up_copy(slot, held.at[slot]).start()

        @pl.when(above < chain)
        def _():
            slot = slot_at(above, which)
            wait_rows(slot)

            @pl.when(has_down)
            def _():
                down_copy(slot, held.at[slot]).start()

    def project(slot):
        store_rows(slot).start()

        @pl.loop(0, weights.shape[1] // 256)
        def _(tile):
            columns = pl.ds(pl.multiple_of(tile * 256, 256), 256)
            partial[slot, :, columns] = jnp.dot(
                held[slot], weights[:, columns], preferred_element_type=jnp.float32)

        partial_copy(slot).start()

    def project_at(distance, which):
        below = place - distance
        above = place + distance

        @pl.when(below >= 0)
        def _():
            project(slot_at(below, which))

        @pl.when(above < chain)
        def _():
            project(slot_at(above, which))

    receive(1, 0)
    receive(1, 1)
    for load in loads:
        load.wait()
    weight_copy.wait_recv()
    shares = []
    for step in range(1, dp_count):
        peer = lax.rem(core + step, dp_count)
        shares.append(pltpu.make_async_remote_copy(
            src_ref=weights.at[share_rows, mate_cols], dst_ref=weights.at[share_rows, mate_cols],
            send_sem=share_send.at[step - 1], recv_sem=share_recv.at[step - 1],
            device_id={"dp": peer}, device_id_type=MESH))
    for copy in shares:
        copy.start()
    for copy in shares:
        copy.wait_recv()

    @pl.loop(0, 2)
    def _(which):
        project(slot_at(place, which))

    @pl.loop(0, 2)
    def _(which):
        project_at(1, which)

    @pl.loop(4, 2 * chain)
    def _(step):
        distance = lax.div(step, 2)
        which = lax.rem(step, 2)
        receive(distance, which)
        project_at(distance, which)

    def finish(slot):
        partial_copy(slot).wait_recv()
        cosine, sine = cosine_sine(table_ref[pl.ds(pl.multiple_of(slot * rows, rows), rows), :])

        def turn(mixed):
            return (mixed * cosine + swap_halves(mixed) * sine).astype(jnp.bfloat16)

        for head in range(heads):
            columns = slice(head * head_width, (head + 1) * head_width)
            shifted = slice((head + 2) * head_width, (head + 3) * head_width)
            queries[slot, head * rows:(head + 1) * rows, :] = turn(
                partial[slot, :, columns] + other[slot, :, shifted])
        pairs[slot, :, :head_width] = turn(
            partial[slot, :, query_cols:query_cols + head_width] + other[slot, :, :head_width])
        pairs[slot, :, head_width:] = (
            partial[slot, :, query_cols + head_width:own_cols]
            + other[slot, :, head_width:2 * head_width]
        ).astype(jnp.bfloat16)
        store_queries(slot).start()
        store_pairs(slot).start()

    @pl.loop(0, 2 * chain)
    def _(step):
        distance = lax.div(step, 2)
        which = lax.rem(step, 2)
        below = place - distance
        above = place + distance

        @pl.when(below >= 0)
        def _():
            finish(slot_at(below, which))

        @pl.when((above < chain) & (distance > 0))
        def _():
            finish(slot_at(above, which))

    store_upstream.wait()
    to_mate.wait_send()
    weight_copy.wait_send()
    for copy in shares:
        copy.wait_send()

    @pl.loop(0, count)
    def _(slot):
        partial_copy(slot).wait_send()
        store_rows(slot).wait()
        store_queries(slot).wait()
        store_pairs(slot).wait()
        origin = lax.div(slot, 2)

        @pl.when(has_up & (origin <= place))
        def _():
            up_copy(slot, held.at[slot]).wait_send()

        @pl.when(has_down & (origin >= place))
        def _():
            down_copy(slot, held.at[slot]).wait_send()


def gather_project(lengths, head_grad, table, hidden, query_weight, key_weight, value_weight):
    count = lax.axis_size("tensor")
    dp_count = lax.axis_size("dp")
    rows, model_width = hidden.shape
    half = model_width // 2
    query_cols = query_weight.shape[1]
    head_width = key_weight.shape[1]
    own_cols = query_cols + 2 * head_width
    all_cols = own_cols + query_cols
    heads = query_cols // head_width
    stack_shape = jax.ShapeDtypeStruct((count, heads * rows, head_width), jnp.bfloat16)
    pair_shape = jax.ShapeDtypeStruct((count, rows, 2 * head_width), jnp.bfloat16)
    dma = pltpu.SemaphoreType.DMA
    anywhere = pl.BlockSpec(memory_space=pl.ANY)
    return pl.pallas_call(
        functools.partial(gather_project_kernel, count, dp_count),
        out_shape=(
            jax.ShapeDtypeStruct((count, rows, half), jnp.bfloat16),
            stack_shape,
            pair_shape,
            stack_shape,
        ),
        in_specs=[pl.BlockSpec(memory_space=pltpu.SMEM)]
        + [pl.BlockSpec(memory_space=pltpu.VMEM)] * 2 + [anywhere] * 4,
        out_specs=(anywhere,) * 4,
        scratch_shapes=[
            pltpu.VMEM((count, rows, half), jnp.bfloat16),
            pltpu.VMEM((half, all_cols), jnp.bfloat16),
            pltpu.VMEM((count, rows, all_cols), jnp.float32),
            pltpu.VMEM((count, rows, own_cols), jnp.float32),
            pltpu.VMEM(stack_shape.shape, jnp.bfloat16),
            pltpu.VMEM(pair_shape.shape, jnp.bfloat16),
            pltpu.VMEM(stack_shape.shape, jnp.bfloat16),
            dma((count,)), dma((count,)), dma((count,)), dma, dma((4,)), dma, dma,
            dma((dp_count - 1,)), dma((dp_count - 1,)), dma((count,)), dma((count,)),
            dma((count,)), dma((count,)), dma((count,)), dma,
        ],
        compiler_params=pltpu.CompilerParams(
            collective_id=0, has_side_effects=True, vmem_limit_bytes=58 * 2**20),
    )(lengths, head_grad, table, hidden, query_weight, key_weight, value_weight)

def attend_kernel(
    dp_count, head_width, queries, upstream, pairs, table_ref, rows_ref,
    squares_out, peer_out,
    rows, grads, mate_grads, rounded, peer_squares,
    rows_load, grad_send, grad_recv, final_send, final_recv, peer_send, peer_recv,
):
    me = lax.axis_index("tensor")
    core = lax.axis_index("dp")
    side = lax.rem(me, 2)
    mate = me + 1 - 2 * side
    blocks, stacked, _ = queries.shape
    step_rows = head_width
    scale = 1.0 / math.sqrt(head_width)
    share = squares_out.shape[1]
    tile = 256
    tiles = share // tile

    barrier = pltpu.get_barrier_semaphore()
    pl.semaphore_signal(barrier, inc=1, device_id={"tensor": mate}, device_id_type=MESH)
    for step in range(1, dp_count):
        peer = lax.rem(core + step, dp_count)
        pl.semaphore_signal(barrier, inc=1, device_id={"dp": peer}, device_id_type=MESH)

    load = pltpu.make_async_copy(rows_ref, rows, rows_load)
    load.start()
    pl.semaphore_wait(barrier, dp_count)

    def grad_copy(block):
        return pltpu.make_async_remote_copy(
            src_ref=grads.at[block], dst_ref=mate_grads.at[block],
            send_sem=grad_send.at[block], recv_sem=grad_recv.at[block],
            device_id={"tensor": mate}, device_id_type=MESH)

    def rows_of(block):
        return slice(block * step_rows, (block + 1) * step_rows)

    def final_copy(block):
        here = rows_of(block)
        return pltpu.make_async_remote_copy(
            src_ref=rounded.at[here], dst_ref=rounded.at[here],
            send_sem=final_send.at[block], recv_sem=final_recv.at[block],
            device_id={"tensor": mate}, device_id_type=MESH)

    def finish(block):
        @pl.when(side == block % 2)
        def _():
            grad_copy(block).wait_recv()
            here = rows_of(block)
            cosine, sine = cosine_sine(table_ref[here, :])
            key_grad = grads[block, :, :head_width] + mate_grads[block, :, :head_width]
            key_grad = key_grad * cosine - swap_halves(key_grad) * sine
            rounded[here, :head_width] = key_grad.astype(jnp.bfloat16)
            rounded[here, head_width:] = (
                grads[block, :, head_width:] + mate_grads[block, :, head_width:]
            ).astype(jnp.bfloat16)
            final_copy(block).start()

    wide = 2 * head_width
    contract_last = (((1,), (1,)), ((), ()))
    for block in reversed(range(blocks)):
        extent = (block + 1) * step_rows
        for chunk in range(stacked // wide):
            chunk_rows = slice(chunk * wide, (chunk + 1) * wide)
            query = queries[block, chunk_rows, :]
            above = upstream[block, chunk_rows, :]
            scores = lax.dot_general(
                pairs[:extent, :head_width], query, contract_last, preferred_element_type=jnp.float32)
            key_at = lax.broadcasted_iota(jnp.int32, (step_rows, wide), 0)
            query_at = lax.rem(lax.broadcasted_iota(jnp.int32, (step_rows, wide), 1), step_rows)
            corner = jnp.where(key_at <= query_at, scores[extent - step_rows:], far_below)
            if block > 0:
                scores = jnp.concatenate([scores[:extent - step_rows], corner], axis=0)
            else:
                scores = corner
            peak = jnp.max(scores, axis=0, keepdims=True)
            powers = jnp.exp((scores - peak) * scale)
            prob = powers * (1.0 / jnp.sum(powers, axis=0, keepdims=True))
            dprob = lax.dot_general(
                pairs[:extent, head_width:], above, contract_last, preferred_element_type=jnp.float32)
            row_dot = jnp.sum(prob * dprob, axis=0, keepdims=True)
            dscore = (prob * (dprob - row_dot) * scale).astype(jnp.bfloat16)
            key_part = jnp.dot(dscore, query, preferred_element_type=jnp.float32)
            value_part = jnp.dot(
                prob.astype(jnp.bfloat16), above, preferred_element_type=jnp.float32)
            key_part = key_part.reshape(block + 1, step_rows, head_width)
            value_part = value_part.reshape(block + 1, step_rows, head_width)
            if block == blocks - 1 and chunk == 0:
                grads[:, :, :head_width] = key_part
                grads[:, :, head_width:] = value_part
            else:
                grads[:block + 1, :, :head_width] += key_part
                grads[:block + 1, :, head_width:] += value_part
        @pl.when(side != block % 2)
        def _():
            grad_copy(block).start()

        if block + 3 < blocks:
            finish(block + 3)

    for block in reversed(range(min(3, blocks))):
        finish(block)
    for block in reversed(range(blocks)):
        @pl.when(side != block % 2)
        def _():
            final_copy(block).wait_recv()

    load.wait()

    def squares_of(start):
        columns = pl.ds(pl.multiple_of(start, tile), tile)
        sample = lax.dot_general(
            rows[:, columns], rounded[...], (((0,), (0,)), ((), ())),
            preferred_element_type=jnp.float32)
        return sample * sample

    def peer_copy(step, index):
        here = pl.ds(pl.multiple_of(index * tile, tile), tile)
        return pltpu.make_async_remote_copy(
            src_ref=peer_squares.at[step - 1, :, here], dst_ref=peer_out.at[step - 1, :, here],
            send_sem=peer_send.at[step - 1, index], recv_sem=peer_recv.at[step - 1, index],
            device_id={"dp": lax.rem(core + step, dp_count)}, device_id_type=MESH)

    for step in range(1, dp_count):
        @pl.loop(0, tiles)
        def _(index):
            here = pl.ds(pl.multiple_of(index * tile, tile), tile)
            start = lax.rem(core + step, dp_count) * share + index * tile
            squares = squares_of(start)
            peer_squares[step - 1, 0, here, :] = squares[:, :head_width]
            peer_squares[step - 1, 1, here, :] = squares[:, head_width:]
            peer_copy(step, index).start()

    @pl.loop(0, tiles)
    def _(index):
        here = pl.ds(pl.multiple_of(index * tile, tile), tile)
        squares = squares_of(core * share + index * tile)
        squares_out[0, here, :] = squares[:, :head_width]
        squares_out[1, here, :] = squares[:, head_width:]

    for block in range(blocks):
        @pl.when(side != block % 2)
        def _():
            grad_copy(block).wait_send()

        @pl.when(side == block % 2)
        def _():
            final_copy(block).wait_send()
    for step in range(1, dp_count):
        @pl.loop(0, tiles)
        def _(index):
            peer_copy(step, index).wait()


def attend(queries, upstream, pairs, table, half_rows, head_width):
    dp_count = lax.axis_size("dp")
    length, half = half_rows.shape
    blocks = length // head_width
    share = half // dp_count
    wide = 2 * head_width
    dma = pltpu.SemaphoreType.DMA
    here = pl.BlockSpec(memory_space=pltpu.VMEM)
    anywhere = pl.BlockSpec(memory_space=pl.ANY)
    return pl.pallas_call(
        functools.partial(attend_kernel, dp_count, head_width),
        out_shape=(
            jax.ShapeDtypeStruct((2, share, head_width), jnp.float32),
            jax.ShapeDtypeStruct((dp_count - 1, 2, share, head_width), jnp.float32),
        ),
        in_specs=[here] * 4 + [anywhere],
        out_specs=(here, anywhere),
        scratch_shapes=[
            pltpu.VMEM((length, half), jnp.bfloat16),
            pltpu.VMEM((blocks, head_width, wide), jnp.float32),
            pltpu.VMEM((blocks, head_width, wide), jnp.float32),
            pltpu.VMEM((length, wide), jnp.bfloat16),
            pltpu.VMEM((dp_count - 1, 2, share, head_width), jnp.float32),
            dma, dma((blocks,)), dma((blocks,)), dma((blocks,)), dma((blocks,)),
            dma((dp_count - 1, share // 256)), dma((dp_count - 1, share // 256)),
        ],
        compiler_params=pltpu.CompilerParams(
            collective_id=1, has_side_effects=True, vmem_limit_bytes=56 * 2**20),
    )(queries, upstream, pairs, table, half_rows)


def local(hidden, query_weight, key_weight, value_weight, head_grad, lengths):
    head_width = key_weight.shape[2]
    length = head_grad.shape[1]
    table = jnp.asarray(turn_table(length, head_width))
    half_rows, queries, pairs, upstream = gather_project(
        lengths, head_grad[0], table, hidden[0], query_weight, key_weight[0], value_weight[0]
    )
    own, peer = attend(
        queries, upstream, pairs.reshape(length, -1), table, half_rows.reshape(length, -1),
        head_width,
    )
    fisher_key = own[:1] + jnp.sum(peer[:, :1], axis=0)
    fisher_value = own[1:] + jnp.sum(peer[:, 1:], axis=0)
    return (fisher_key, fisher_value)


def solution(mesh):
    in_specs = (
        P(("groups", "dp"), "tensor", None),
        P(None, "tensor"),
        P("tensor", None, None),
        P("tensor", None, None),
        P(("groups", "dp"), None, "tensor"),
        P(("groups", "dp")),
    )
    out_specs = (P(("groups", "tensor"), "dp", None), P(("groups", "tensor"), "dp", None))
    return jax.shard_map(local, mesh=mesh, in_specs=in_specs, out_specs=out_specs, check_vma=False)
```

```python
import functools
import math

import jax
import jax.numpy as jnp
import numpy as np
from jax import lax
from jax.experimental import pallas as pl
from jax.experimental.pallas import tpu as pltpu
from jax.sharding import PartitionSpec as P

MESH = pl.DeviceIdType.MESH

rope_base = 1000000.0
far_below = -1e30


def turn_table(length, head_width):
    position = np.arange(length, dtype=np.float64)[:, None]
    frequency = rope_base ** (-2.0 * np.arange(head_width // 2, dtype=np.float64) / head_width)
    angles = position * frequency
    return np.concatenate([np.cos(angles), np.sin(angles)], axis=-1).astype(np.float32)


def swap_halves(vectors):
    return pltpu.roll(vectors, vectors.shape[-1] // 2, axis=1)


def cosine_sine(table):
    other = swap_halves(table)
    lead = lax.broadcasted_iota(jnp.int32, table.shape, 1) < table.shape[1] // 2
    return jnp.where(lead, table, other), jnp.where(lead, -other, table)


def gather_project_kernel(
    count, dp_count, lengths_ref, gradient_ref, table_ref,
    hidden_ref, query_ref, key_ref, value_ref,
    rows_out, queries_out, pairs_out, upstream_out,
    held, weights, partial, other, queries, pairs, upstream,
    rows_recv, up_send, down_send, mate_send, load_sem, weight_send, weight_recv,
    share_send, share_recv, partial_send, partial_recv, rows_store, queries_store, pairs_store,
    upstream_store,
):
    me = lax.axis_index("tensor")
    core = lax.axis_index("dp")
    side = lax.rem(me, 2)
    place = lax.div(me, 2)
    mate = me + 1 - 2 * side
    chain = count // 2
    half = held.shape[2]
    query_cols = query_ref.shape[1]
    head_width = key_ref.shape[1]
    own_cols = query_cols + 2 * head_width
    has_up = place < chain - 1
    has_down = place > 0
    share = half // dp_count

    barrier = pltpu.get_barrier_semaphore()
    pl.semaphore_signal(barrier, inc=1, device_id={"tensor": mate}, device_id_type=MESH)
    for step in range(1, dp_count):
        peer = lax.rem(core + step, dp_count)
        pl.semaphore_signal(barrier, inc=1, device_id={"dp": peer}, device_id_type=MESH)

    @pl.when(has_up)
    def _():
        pl.semaphore_signal(barrier, inc=1, device_id={"tensor": me + 2}, device_id_type=MESH)

    @pl.when(has_down)
    def _():
        pl.semaphore_signal(barrier, inc=1, device_id={"tensor": me - 2}, device_id_type=MESH)

    edges = jnp.where(has_up, 1, 0) + jnp.where(has_down, 1, 0)
    pl.semaphore_wait(barrier, dp_count + edges)

    own_half = hidden_ref.at[:, pl.ds(pl.multiple_of(side * half, half), half)]
    mate_half = hidden_ref.at[:, pl.ds(pl.multiple_of((1 - side) * half, half), half)]

    def up_copy(slot, source):
        return pltpu.make_async_remote_copy(
            src_ref=source, dst_ref=held.at[slot], send_sem=up_send.at[slot],
            recv_sem=rows_recv.at[slot], device_id={"tensor": me + 2}, device_id_type=MESH)

    def down_copy(slot, source):
        return pltpu.make_async_remote_copy(
            src_ref=source, dst_ref=held.at[slot], send_sem=down_send.at[slot],
            recv_sem=rows_recv.at[slot], device_id={"tensor": me - 2}, device_id_type=MESH)

    def wait_rows(slot):
        pltpu.make_async_remote_copy(
            src_ref=held.at[slot], dst_ref=held.at[slot], send_sem=mate_send,
            recv_sem=rows_recv.at[slot], device_id={"tensor": mate}, device_id_type=MESH).wait_recv()

    def store_rows(slot):
        return pltpu.make_async_copy(held.at[slot], rows_out.at[slot], rows_store.at[slot])

    def store_queries(slot):
        return pltpu.make_async_copy(queries.at[slot], queries_out.at[slot], queries_store.at[slot])

    def store_pairs(slot):
        return pltpu.make_async_copy(pairs.at[slot], pairs_out.at[slot], pairs_store.at[slot])

    tile = 256
    pieces = own_cols // tile

    def partial_copy(slot, piece):
        source = pl.ds(pl.multiple_of(query_cols + piece * tile, tile), tile)
        target = pl.ds(pl.multiple_of(piece * tile, tile), tile)
        return pltpu.make_async_remote_copy(
            src_ref=partial.at[slot, :, source], dst_ref=other.at[slot, :, target],
            send_sem=partial_send.at[slot, piece], recv_sem=partial_recv.at[slot, piece],
            device_id={"tensor": mate}, device_id_type=MESH)

    to_mate = pltpu.make_async_remote_copy(
        src_ref=mate_half, dst_ref=held.at[me], send_sem=mate_send,
        recv_sem=rows_recv.at[me], device_id={"tensor": mate}, device_id_type=MESH)
    to_mate.start()

    @pl.when(has_up)
    def _():
        up_copy(me, own_half).start()

    @pl.when(has_down)
    def _():
        down_copy(me, own_half).start()

    half_rows = pl.ds(pl.multiple_of(side * half, half), half)
    loads = [
        pltpu.make_async_copy(own_half, held.at[me], load_sem.at[0]),
        pltpu.make_async_copy(
            query_ref.at[half_rows], weights.at[:, pl.ds(0, query_cols)], load_sem.at[1]),
        pltpu.make_async_copy(
            key_ref, weights.at[:, pl.ds(query_cols, head_width)], load_sem.at[2]),
        pltpu.make_async_copy(
            value_ref, weights.at[:, pl.ds(query_cols + head_width, head_width)], load_sem.at[3]),
    ]
    for load in loads:
        load.start()

    share_rows = pl.ds(pl.multiple_of(core * share, share), share)
    mate_cols = pl.ds(own_cols, query_cols)
    weight_copy = pltpu.make_async_remote_copy(
        src_ref=query_ref.at[pl.ds(pl.multiple_of((1 - side) * half + core * share, share), share)],
        dst_ref=weights.at[share_rows, mate_cols], send_sem=weight_send, recv_sem=weight_recv,
        device_id={"tensor": mate}, device_id_type=MESH)

    live = lengths_ref[0]
    rows = held.shape[1]
    heads = query_cols // head_width

    @pl.loop(0, count)
    def _(slot):
        here = pl.ds(pl.multiple_of(slot * rows, rows), rows)
        position = slot * rows + lax.broadcasted_iota(jnp.int32, (rows, head_width), 0)
        for head in range(heads):
            gradient = gradient_ref[here, head * head_width:(head + 1) * head_width]
            upstream[slot, head * rows:(head + 1) * rows, :] = jnp.where(
                position < live, gradient.astype(jnp.float32), 0.0).astype(jnp.bfloat16)

    store_upstream = pltpu.make_async_copy(upstream, upstream_out, upstream_store)
    store_upstream.start()
    wait_rows(mate)

    @pl.when(has_up)
    def _():
        up_copy(mate, held.at[mate]).start()

    @pl.when(has_down)
    def _():
        down_copy(mate, held.at[mate]).start()

    weight_copy.start()

    def slot_at(step, which):
        return 2 * step + jnp.where(which == 0, side, 1 - side)

    def receive(distance, which):
        below = place - distance
        above = place + distance

        @pl.when(below >= 0)
        def _():
            slot = slot_at(below, which)
            wait_rows(slot)

            @pl.when(has_up)
            def _():
                up_copy(slot, held.at[slot]).start()

        @pl.when(above < chain)
        def _():
            slot = slot_at(above, which)
            wait_rows(slot)

            @pl.when(has_down)
            def _():
                down_copy(slot, held.at[slot]).start()

    def project(slot):
        store_rows(slot).start()

        def multiply(start):
            columns = pl.ds(pl.multiple_of(start, tile), tile)
            partial[slot, :, columns] = jnp.dot(
                held[slot], weights[:, columns], preferred_element_type=jnp.float32)

        @pl.loop(0, pieces)
        def _(piece):
            multiply(query_cols + piece * tile)
            partial_copy(slot, piece).start()

        @pl.loop(0, query_cols // tile)
        def _(piece):
            multiply(piece * tile)

    def project_at(distance, which):
        below = place - distance
        above = place + distance

        @pl.when(below >= 0)
        def _():
            project(slot_at(below, which))

        @pl.when(above < chain)
        def _():
            project(slot_at(above, which))

    receive(1, 0)
    receive(1, 1)
    for load in loads:
        load.wait()
    weight_copy.wait_recv()
    shares = []
    for step in range(1, dp_count):
        peer = lax.rem(core + step, dp_count)
        shares.append(pltpu.make_async_remote_copy(
            src_ref=weights.at[share_rows, mate_cols], dst_ref=weights.at[share_rows, mate_cols],
            send_sem=share_send.at[step - 1], recv_sem=share_recv.at[step - 1],
            device_id={"dp": peer}, device_id_type=MESH))
    for copy in shares:
        copy.start()
    for copy in shares:
        copy.wait_recv()

    @pl.loop(0, 2)
    def _(which):
        project(slot_at(place, which))

    @pl.loop(0, 2)
    def _(which):
        project_at(1, which)

    @pl.loop(4, 2 * chain)
    def _(step):
        distance = lax.div(step, 2)
        which = lax.rem(step, 2)
        receive(distance, which)
        project_at(distance, which)

    def finish(slot):
        for piece in range(pieces):
            partial_copy(slot, piece).wait_recv()
        cosine, sine = cosine_sine(table_ref[pl.ds(pl.multiple_of(slot * rows, rows), rows), :])

        def turn(mixed):
            return (mixed * cosine + swap_halves(mixed) * sine).astype(jnp.bfloat16)

        for head in range(heads):
            columns = slice(head * head_width, (head + 1) * head_width)
            shifted = slice((head + 2) * head_width, (head + 3) * head_width)
            queries[slot, head * rows:(head + 1) * rows, :] = turn(
                partial[slot, :, columns] + other[slot, :, shifted])
        pairs[slot, :, :head_width] = turn(
            partial[slot, :, query_cols:query_cols + head_width] + other[slot, :, :head_width])
        pairs[slot, :, head_width:] = (
            partial[slot, :, query_cols + head_width:own_cols]
            + other[slot, :, head_width:2 * head_width]
        ).astype(jnp.bfloat16)
        store_queries(slot).start()
        store_pairs(slot).start()

    @pl.loop(0, 2 * chain)
    def _(step):
        distance = lax.div(step, 2)
        which = lax.rem(step, 2)
        below = place - distance
        above = place + distance

        @pl.when(below >= 0)
        def _():
            finish(slot_at(below, which))

        @pl.when((above < chain) & (distance > 0))
        def _():
            finish(slot_at(above, which))

    store_upstream.wait()
    to_mate.wait_send()
    weight_copy.wait_send()
    for copy in shares:
        copy.wait_send()

    @pl.loop(0, count)
    def _(slot):
        for piece in range(pieces):
            partial_copy(slot, piece).wait_send()
        store_rows(slot).wait()
        store_queries(slot).wait()
        store_pairs(slot).wait()
        origin = lax.div(slot, 2)

        @pl.when(has_up & (origin <= place))
        def _():
            up_copy(slot, held.at[slot]).wait_send()

        @pl.when(has_down & (origin >= place))
        def _():
            down_copy(slot, held.at[slot]).wait_send()


def gather_project(lengths, head_grad, table, hidden, query_weight, key_weight, value_weight):
    count = lax.axis_size("tensor")
    dp_count = lax.axis_size("dp")
    rows, model_width = hidden.shape
    half = model_width // 2
    query_cols = query_weight.shape[1]
    head_width = key_weight.shape[1]
    own_cols = query_cols + 2 * head_width
    all_cols = own_cols + query_cols
    heads = query_cols // head_width
    stack_shape = jax.ShapeDtypeStruct((count, heads * rows, head_width), jnp.bfloat16)
    pair_shape = jax.ShapeDtypeStruct((count, rows, 2 * head_width), jnp.bfloat16)
    dma = pltpu.SemaphoreType.DMA
    anywhere = pl.BlockSpec(memory_space=pl.ANY)
    return pl.pallas_call(
        functools.partial(gather_project_kernel, count, dp_count),
        out_shape=(
            jax.ShapeDtypeStruct((count, rows, half), jnp.bfloat16),
            stack_shape,
            pair_shape,
            stack_shape,
        ),
        in_specs=[pl.BlockSpec(memory_space=pltpu.SMEM)]
        + [pl.BlockSpec(memory_space=pltpu.VMEM)] * 2 + [anywhere] * 4,
        out_specs=(anywhere,) * 4,
        scratch_shapes=[
            pltpu.VMEM((count, rows, half), jnp.bfloat16),
            pltpu.VMEM((half, all_cols), jnp.bfloat16),
            pltpu.VMEM((count, rows, all_cols), jnp.float32),
            pltpu.VMEM((count, rows, own_cols), jnp.float32),
            pltpu.VMEM(stack_shape.shape, jnp.bfloat16),
            pltpu.VMEM(pair_shape.shape, jnp.bfloat16),
            pltpu.VMEM(stack_shape.shape, jnp.bfloat16),
            dma((count,)), dma((count,)), dma((count,)), dma, dma((4,)), dma, dma,
            dma((dp_count - 1,)), dma((dp_count - 1,)),
            dma((count, own_cols // 256)), dma((count, own_cols // 256)),
            dma((count,)), dma((count,)), dma((count,)), dma,
        ],
        compiler_params=pltpu.CompilerParams(
            collective_id=0, has_side_effects=True, vmem_limit_bytes=58 * 2**20),
    )(lengths, head_grad, table, hidden, query_weight, key_weight, value_weight)

def attend_kernel(
    dp_count, head_width, queries, upstream, pairs, table_ref, rows_ref,
    squares_out, peer_out,
    rows, grads, mate_grads, rounded, peer_squares,
    rows_load, grad_send, grad_recv, final_send, final_recv, peer_send, peer_recv,
):
    me = lax.axis_index("tensor")
    core = lax.axis_index("dp")
    side = lax.rem(me, 2)
    mate = me + 1 - 2 * side
    blocks, stacked, _ = queries.shape
    step_rows = head_width
    scale = 1.0 / math.sqrt(head_width)
    share = squares_out.shape[1]
    tile = 256
    tiles = share // tile

    barrier = pltpu.get_barrier_semaphore()
    pl.semaphore_signal(barrier, inc=1, device_id={"tensor": mate}, device_id_type=MESH)
    for step in range(1, dp_count):
        peer = lax.rem(core + step, dp_count)
        pl.semaphore_signal(barrier, inc=1, device_id={"dp": peer}, device_id_type=MESH)

    load = pltpu.make_async_copy(rows_ref, rows, rows_load)
    load.start()
    pl.semaphore_wait(barrier, dp_count)

    def grad_copy(block):
        return pltpu.make_async_remote_copy(
            src_ref=grads.at[block], dst_ref=mate_grads.at[block],
            send_sem=grad_send.at[block], recv_sem=grad_recv.at[block],
            device_id={"tensor": mate}, device_id_type=MESH)

    def rows_of(block):
        return slice(block * step_rows, (block + 1) * step_rows)

    def final_copy(block):
        here = rows_of(block)
        return pltpu.make_async_remote_copy(
            src_ref=rounded.at[here], dst_ref=rounded.at[here],
            send_sem=final_send.at[block], recv_sem=final_recv.at[block],
            device_id={"tensor": mate}, device_id_type=MESH)

    def finish(block):
        @pl.when(side == block % 2)
        def _():
            grad_copy(block).wait_recv()
            here = rows_of(block)
            cosine, sine = cosine_sine(table_ref[here, :])
            key_grad = grads[block, :, :head_width] + mate_grads[block, :, :head_width]
            key_grad = key_grad * cosine - swap_halves(key_grad) * sine
            rounded[here, :head_width] = key_grad.astype(jnp.bfloat16)
            rounded[here, head_width:] = (
                grads[block, :, head_width:] + mate_grads[block, :, head_width:]
            ).astype(jnp.bfloat16)
            final_copy(block).start()

    wide = 2 * head_width
    contract_last = (((1,), (1,)), ((), ()))
    for block in reversed(range(blocks)):
        extent = (block + 1) * step_rows
        for chunk in range(stacked // wide):
            chunk_rows = slice(chunk * wide, (chunk + 1) * wide)
            query = queries[block, chunk_rows, :]
            above = upstream[block, chunk_rows, :]
            scores = lax.dot_general(
                pairs[:extent, :head_width], query, contract_last, preferred_element_type=jnp.float32)
            key_at = lax.broadcasted_iota(jnp.int32, (step_rows, wide), 0)
            query_at = lax.rem(lax.broadcasted_iota(jnp.int32, (step_rows, wide), 1), step_rows)
            corner = jnp.where(key_at <= query_at, scores[extent - step_rows:], far_below)
            if block > 0:
                scores = jnp.concatenate([scores[:extent - step_rows], corner], axis=0)
            else:
                scores = corner
            peak = jnp.max(scores, axis=0, keepdims=True)
            powers = jnp.exp2((scores - peak) * (scale * math.log2(math.e)))
            prob = powers * (1.0 / jnp.sum(powers, axis=0, keepdims=True))
            dprob = lax.dot_general(
                pairs[:extent, head_width:], above, contract_last, preferred_element_type=jnp.float32)
            row_dot = jnp.sum(prob * dprob, axis=0, keepdims=True)
            dscore = (prob * (dprob - row_dot) * scale).astype(jnp.bfloat16)
            key_part = jnp.dot(dscore, query, preferred_element_type=jnp.float32)
            value_part = jnp.dot(
                prob.astype(jnp.bfloat16), above, preferred_element_type=jnp.float32)
            key_part = key_part.reshape(block + 1, step_rows, head_width)
            value_part = value_part.reshape(block + 1, step_rows, head_width)
            if block == blocks - 1 and chunk == 0:
                grads[:, :, :head_width] = key_part
                grads[:, :, head_width:] = value_part
            else:
                grads[:block + 1, :, :head_width] += key_part
                grads[:block + 1, :, head_width:] += value_part
        @pl.when(side != block % 2)
        def _():
            grad_copy(block).start()

        if block + 3 < blocks:
            finish(block + 3)

    for block in reversed(range(min(3, blocks))):
        finish(block)
    for block in reversed(range(blocks)):
        @pl.when(side != block % 2)
        def _():
            final_copy(block).wait_recv()

    load.wait()

    def squares_of(start):
        columns = pl.ds(pl.multiple_of(start, tile), tile)
        sample = lax.dot_general(
            rows[:, columns], rounded[...], (((0,), (0,)), ((), ())),
            preferred_element_type=jnp.float32)
        return sample * sample

    def peer_copy(step, index):
        here = pl.ds(pl.multiple_of(index * tile, tile), tile)
        return pltpu.make_async_remote_copy(
            src_ref=peer_squares.at[step - 1, :, here], dst_ref=peer_out.at[step - 1, :, here],
            send_sem=peer_send.at[step - 1, index], recv_sem=peer_recv.at[step - 1, index],
            device_id={"dp": lax.rem(core + step, dp_count)}, device_id_type=MESH)

    for step in range(1, dp_count):
        @pl.loop(0, tiles)
        def _(index):
            here = pl.ds(pl.multiple_of(index * tile, tile), tile)
            start = lax.rem(core + step, dp_count) * share + index * tile
            squares = squares_of(start)
            peer_squares[step - 1, 0, here, :] = squares[:, :head_width]
            peer_squares[step - 1, 1, here, :] = squares[:, head_width:]
            peer_copy(step, index).start()

    @pl.loop(0, tiles)
    def _(index):
        here = pl.ds(pl.multiple_of(index * tile, tile), tile)
        squares = squares_of(core * share + index * tile)
        squares_out[0, here, :] = squares[:, :head_width]
        squares_out[1, here, :] = squares[:, head_width:]

    for block in range(blocks):
        @pl.when(side != block % 2)
        def _():
            grad_copy(block).wait_send()

        @pl.when(side == block % 2)
        def _():
            final_copy(block).wait_send()
    for step in range(1, dp_count):
        @pl.loop(0, tiles)
        def _(index):
            peer_copy(step, index).wait()


def attend(queries, upstream, pairs, table, half_rows, head_width):
    dp_count = lax.axis_size("dp")
    length, half = half_rows.shape
    blocks = length // head_width
    share = half // dp_count
    wide = 2 * head_width
    dma = pltpu.SemaphoreType.DMA
    here = pl.BlockSpec(memory_space=pltpu.VMEM)
    anywhere = pl.BlockSpec(memory_space=pl.ANY)
    return pl.pallas_call(
        functools.partial(attend_kernel, dp_count, head_width),
        out_shape=(
            jax.ShapeDtypeStruct((2, share, head_width), jnp.float32),
            jax.ShapeDtypeStruct((dp_count - 1, 2, share, head_width), jnp.float32),
        ),
        in_specs=[here] * 4 + [anywhere],
        out_specs=(here, anywhere),
        scratch_shapes=[
            pltpu.VMEM((length, half), jnp.bfloat16),
            pltpu.VMEM((blocks, head_width, wide), jnp.float32),
            pltpu.VMEM((blocks, head_width, wide), jnp.float32),
            pltpu.VMEM((length, wide), jnp.bfloat16),
            pltpu.VMEM((dp_count - 1, 2, share, head_width), jnp.float32),
            dma, dma((blocks,)), dma((blocks,)), dma((blocks,)), dma((blocks,)),
            dma((dp_count - 1, share // 256)), dma((dp_count - 1, share // 256)),
        ],
        compiler_params=pltpu.CompilerParams(
            collective_id=1, has_side_effects=True, vmem_limit_bytes=56 * 2**20),
    )(queries, upstream, pairs, table, half_rows)


def local(hidden, query_weight, key_weight, value_weight, head_grad, lengths):
    head_width = key_weight.shape[2]
    length = head_grad.shape[1]
    table = jnp.asarray(turn_table(length, head_width))
    half_rows, queries, pairs, upstream = gather_project(
        lengths, head_grad[0], table, hidden[0], query_weight, key_weight[0], value_weight[0]
    )
    own, peer = attend(
        queries, upstream, pairs.reshape(length, -1), table, half_rows.reshape(length, -1),
        head_width,
    )
    fisher_key = own[:1] + jnp.sum(peer[:, :1], axis=0)
    fisher_value = own[1:] + jnp.sum(peer[:, 1:], axis=0)
    return (fisher_key, fisher_value)


def solution(mesh):
    in_specs = (
        P(("groups", "dp"), "tensor", None),
        P(None, "tensor"),
        P("tensor", None, None),
        P("tensor", None, None),
        P(("groups", "dp"), None, "tensor"),
        P(("groups", "dp")),
    )
    out_specs = (P(("groups", "tensor"), "dp", None), P(("groups", "tensor"), "dp", None))
    return jax.shard_map(local, mesh=mesh, in_specs=in_specs, out_specs=out_specs, check_vma=False)
```

```python
import functools
import math

import jax
import jax.numpy as jnp
import numpy as np
from jax import lax
from jax.experimental import pallas as pl
from jax.experimental.pallas import tpu as pltpu
from jax.sharding import PartitionSpec as P

MESH = pl.DeviceIdType.MESH

rope_base = 1000000.0
far_below = -1e30


def turn_table(length, head_width):
    position = np.arange(length, dtype=np.float64)[:, None]
    frequency = rope_base ** (-2.0 * np.arange(head_width // 2, dtype=np.float64) / head_width)
    angles = position * frequency
    return np.concatenate([np.cos(angles), np.sin(angles)], axis=-1).astype(np.float32)


def swap_halves(vectors):
    return pltpu.roll(vectors, vectors.shape[-1] // 2, axis=1)


def cosine_sine(table):
    other = swap_halves(table)
    lead = lax.broadcasted_iota(jnp.int32, table.shape, 1) < table.shape[1] // 2
    return jnp.where(lead, table, other), jnp.where(lead, -other, table)


def gather_project_kernel(
    count, dp_count, lengths_ref, gradient_ref, table_ref,
    hidden_ref, query_ref, key_ref, value_ref,
    rows_out, queries_out, pairs_out, upstream_out,
    held, weights, partial, other, queries, pairs, upstream,
    rows_recv, up_send, down_send, mate_send, load_sem, weight_send, weight_recv,
    share_send, share_recv, partial_send, partial_recv, rows_store, queries_store, pairs_store,
    upstream_store,
):
    me = lax.axis_index("tensor")
    core = lax.axis_index("dp")
    side = lax.rem(me, 2)
    place = lax.div(me, 2)
    mate = me + 1 - 2 * side
    chain = count // 2
    half = held.shape[2]
    query_cols = query_ref.shape[1]
    head_width = key_ref.shape[1]
    own_cols = query_cols + 2 * head_width
    has_up = place < chain - 1
    has_down = place > 0
    share = half // dp_count

    barrier = pltpu.get_barrier_semaphore()
    pl.semaphore_signal(barrier, inc=1, device_id={"tensor": mate}, device_id_type=MESH)
    for step in range(1, dp_count):
        peer = lax.rem(core + step, dp_count)
        pl.semaphore_signal(barrier, inc=1, device_id={"dp": peer}, device_id_type=MESH)

    @pl.when(has_up)
    def _():
        pl.semaphore_signal(barrier, inc=1, device_id={"tensor": me + 2}, device_id_type=MESH)

    @pl.when(has_down)
    def _():
        pl.semaphore_signal(barrier, inc=1, device_id={"tensor": me - 2}, device_id_type=MESH)

    edges = jnp.where(has_up, 1, 0) + jnp.where(has_down, 1, 0)
    pl.semaphore_wait(barrier, dp_count + edges)

    own_half = hidden_ref.at[:, pl.ds(pl.multiple_of(side * half, half), half)]
    mate_half = hidden_ref.at[:, pl.ds(pl.multiple_of((1 - side) * half, half), half)]

    def up_copy(slot, source):
        return pltpu.make_async_remote_copy(
            src_ref=source, dst_ref=held.at[slot], send_sem=up_send.at[slot],
            recv_sem=rows_recv.at[slot], device_id={"tensor": me + 2}, device_id_type=MESH)

    def down_copy(slot, source):
        return pltpu.make_async_remote_copy(
            src_ref=source, dst_ref=held.at[slot], send_sem=down_send.at[slot],
            recv_sem=rows_recv.at[slot], device_id={"tensor": me - 2}, device_id_type=MESH)

    def wait_rows(slot):
        pltpu.make_async_remote_copy(
            src_ref=held.at[slot], dst_ref=held.at[slot], send_sem=mate_send,
            recv_sem=rows_recv.at[slot], device_id={"tensor": mate}, device_id_type=MESH).wait_recv()

    def store_rows(slot):
        return pltpu.make_async_copy(held.at[slot], rows_out.at[slot], rows_store.at[slot])

    def store_queries(slot):
        return pltpu.make_async_copy(queries.at[slot], queries_out.at[slot], queries_store.at[slot])

    def store_pairs(slot):
        return pltpu.make_async_copy(pairs.at[slot], pairs_out.at[slot], pairs_store.at[slot])

    tile = 256
    pieces = own_cols // tile

    def partial_copy(slot, piece):
        source = pl.ds(pl.multiple_of(query_cols + piece * tile, tile), tile)
        target = pl.ds(pl.multiple_of(piece * tile, tile), tile)
        return pltpu.make_async_remote_copy(
            src_ref=partial.at[slot, :, source], dst_ref=other.at[slot, :, target],
            send_sem=partial_send.at[slot, piece], recv_sem=partial_recv.at[slot, piece],
            device_id={"tensor": mate}, device_id_type=MESH)

    to_mate = pltpu.make_async_remote_copy(
        src_ref=mate_half, dst_ref=held.at[me], send_sem=mate_send,
        recv_sem=rows_recv.at[me], device_id={"tensor": mate}, device_id_type=MESH)
    to_mate.start()

    @pl.when(has_up)
    def _():
        up_copy(me, own_half).start()

    @pl.when(has_down)
    def _():
        down_copy(me, own_half).start()

    half_rows = pl.ds(pl.multiple_of(side * half, half), half)
    loads = [
        pltpu.make_async_copy(own_half, held.at[me], load_sem.at[0]),
        pltpu.make_async_copy(
            query_ref.at[half_rows], weights.at[:, pl.ds(0, query_cols)], load_sem.at[1]),
        pltpu.make_async_copy(
            key_ref, weights.at[:, pl.ds(query_cols, head_width)], load_sem.at[2]),
        pltpu.make_async_copy(
            value_ref, weights.at[:, pl.ds(query_cols + head_width, head_width)], load_sem.at[3]),
    ]
    for load in loads:
        load.start()

    share_rows = pl.ds(pl.multiple_of(core * share, share), share)
    mate_cols = pl.ds(own_cols, query_cols)
    weight_copy = pltpu.make_async_remote_copy(
        src_ref=query_ref.at[pl.ds(pl.multiple_of((1 - side) * half + core * share, share), share)],
        dst_ref=weights.at[share_rows, mate_cols], send_sem=weight_send, recv_sem=weight_recv,
        device_id={"tensor": mate}, device_id_type=MESH)

    live = lengths_ref[0]
    rows = held.shape[1]
    heads = query_cols // head_width

    @pl.loop(0, count)
    def _(slot):
        here = pl.ds(pl.multiple_of(slot * rows, rows), rows)
        position = slot * rows + lax.broadcasted_iota(jnp.int32, (rows, head_width), 0)
        for head in range(heads):
            gradient = gradient_ref[here, head * head_width:(head + 1) * head_width]
            upstream[slot, head * rows:(head + 1) * rows, :] = jnp.where(
                position < live, gradient.astype(jnp.float32), 0.0).astype(jnp.bfloat16)

    store_upstream = pltpu.make_async_copy(upstream, upstream_out, upstream_store)
    store_upstream.start()
    wait_rows(mate)

    @pl.when(has_up)
    def _():
        up_copy(mate, held.at[mate]).start()

    @pl.when(has_down)
    def _():
        down_copy(mate, held.at[mate]).start()

    weight_copy.start()

    def slot_at(step, which):
        return 2 * step + jnp.where(which == 0, side, 1 - side)

    def receive(distance, which):
        below = place - distance
        above = place + distance

        @pl.when(below >= 0)
        def _():
            slot = slot_at(below, which)
            wait_rows(slot)

            @pl.when(has_up)
            def _():
                up_copy(slot, held.at[slot]).start()

        @pl.when(above < chain)
        def _():
            slot = slot_at(above, which)
            wait_rows(slot)

            @pl.when(has_down)
            def _():
                down_copy(slot, held.at[slot]).start()

    def multiply(slot, start):
        columns = pl.ds(pl.multiple_of(start, tile), tile)
        partial[slot, :, columns] = jnp.dot(
            held[slot], weights[:, columns], preferred_element_type=jnp.float32)

    def project_pair(slot):
        store_rows(slot).start()
        multiply(slot, query_cols)

    def send_pair(slot):
        partial_copy(slot, 0).start()

    def project_queries(slot):
        @pl.loop(1, pieces)
        def _(piece):
            multiply(slot, query_cols + piece * tile)
            partial_copy(slot, piece).start()

        @pl.loop(0, query_cols // tile)
        def _(piece):
            multiply(slot, piece * tile)

    def project(slot):
        project_pair(slot)
        send_pair(slot)
        project_queries(slot)

    def project_at(distance, which, action):
        below = place - distance
        above = place + distance

        @pl.when(below >= 0)
        def _():
            action(slot_at(below, which))

        @pl.when(above < chain)
        def _():
            action(slot_at(above, which))

    receive(1, 0)
    receive(1, 1)
    for load in loads:
        load.wait()

    def early(action):
        @pl.loop(0, 2)
        def _(which):
            action(slot_at(place, which))

        @pl.loop(0, 2)
        def _(which):
            project_at(1, which, action)

    early(project_pair)
    weight_copy.wait_recv()
    shares = []
    for step in range(1, dp_count):
        peer = lax.rem(core + step, dp_count)
        shares.append(pltpu.make_async_remote_copy(
            src_ref=weights.at[share_rows, mate_cols], dst_ref=weights.at[share_rows, mate_cols],
            send_sem=share_send.at[step - 1], recv_sem=share_recv.at[step - 1],
            device_id={"dp": peer}, device_id_type=MESH))
    for copy in shares:
        copy.start()
    early(send_pair)
    for copy in shares:
        copy.wait_recv()
    early(project_queries)

    @pl.loop(4, 2 * chain)
    def _(step):
        distance = lax.div(step, 2)
        which = lax.rem(step, 2)
        receive(distance, which)
        project_at(distance, which, project)

    def finish(slot):
        for piece in range(pieces):
            partial_copy(slot, piece).wait_recv()
        cosine, sine = cosine_sine(table_ref[pl.ds(pl.multiple_of(slot * rows, rows), rows), :])

        def turn(mixed):
            return (mixed * cosine + swap_halves(mixed) * sine).astype(jnp.bfloat16)

        for head in range(heads):
            columns = slice(head * head_width, (head + 1) * head_width)
            shifted = slice((head + 2) * head_width, (head + 3) * head_width)
            queries[slot, head * rows:(head + 1) * rows, :] = turn(
                partial[slot, :, columns] + other[slot, :, shifted])
        pairs[slot, :, :head_width] = turn(
            partial[slot, :, query_cols:query_cols + head_width] + other[slot, :, :head_width])
        pairs[slot, :, head_width:] = (
            partial[slot, :, query_cols + head_width:own_cols]
            + other[slot, :, head_width:2 * head_width]
        ).astype(jnp.bfloat16)
        store_queries(slot).start()
        store_pairs(slot).start()

    @pl.loop(0, 2 * chain)
    def _(step):
        distance = lax.div(step, 2)
        which = lax.rem(step, 2)
        below = place - distance
        above = place + distance

        @pl.when(below >= 0)
        def _():
            finish(slot_at(below, which))

        @pl.when((above < chain) & (distance > 0))
        def _():
            finish(slot_at(above, which))

    store_upstream.wait()
    to_mate.wait_send()
    weight_copy.wait_send()
    for copy in shares:
        copy.wait_send()

    @pl.loop(0, count)
    def _(slot):
        for piece in range(pieces):
            partial_copy(slot, piece).wait_send()
        store_rows(slot).wait()
        store_queries(slot).wait()
        store_pairs(slot).wait()
        origin = lax.div(slot, 2)

        @pl.when(has_up & (origin <= place))
        def _():
            up_copy(slot, held.at[slot]).wait_send()

        @pl.when(has_down & (origin >= place))
        def _():
            down_copy(slot, held.at[slot]).wait_send()


def gather_project(lengths, head_grad, table, hidden, query_weight, key_weight, value_weight):
    count = lax.axis_size("tensor")
    dp_count = lax.axis_size("dp")
    rows, model_width = hidden.shape
    half = model_width // 2
    query_cols = query_weight.shape[1]
    head_width = key_weight.shape[1]
    own_cols = query_cols + 2 * head_width
    all_cols = own_cols + query_cols
    heads = query_cols // head_width
    stack_shape = jax.ShapeDtypeStruct((count, heads * rows, head_width), jnp.bfloat16)
    pair_shape = jax.ShapeDtypeStruct((count, rows, 2 * head_width), jnp.bfloat16)
    dma = pltpu.SemaphoreType.DMA
    anywhere = pl.BlockSpec(memory_space=pl.ANY)
    return pl.pallas_call(
        functools.partial(gather_project_kernel, count, dp_count),
        out_shape=(
            jax.ShapeDtypeStruct((count, rows, half), jnp.bfloat16),
            stack_shape,
            pair_shape,
            stack_shape,
        ),
        in_specs=[pl.BlockSpec(memory_space=pltpu.SMEM)]
        + [pl.BlockSpec(memory_space=pltpu.VMEM)] * 2 + [anywhere] * 4,
        out_specs=(anywhere,) * 4,
        scratch_shapes=[
            pltpu.VMEM((count, rows, half), jnp.bfloat16),
            pltpu.VMEM((half, all_cols), jnp.bfloat16),
            pltpu.VMEM((count, rows, all_cols), jnp.float32),
            pltpu.VMEM((count, rows, own_cols), jnp.float32),
            pltpu.VMEM(stack_shape.shape, jnp.bfloat16),
            pltpu.VMEM(pair_shape.shape, jnp.bfloat16),
            pltpu.VMEM(stack_shape.shape, jnp.bfloat16),
            dma((count,)), dma((count,)), dma((count,)), dma, dma((4,)), dma, dma,
            dma((dp_count - 1,)), dma((dp_count - 1,)),
            dma((count, own_cols // 256)), dma((count, own_cols // 256)),
            dma((count,)), dma((count,)), dma((count,)), dma,
        ],
        compiler_params=pltpu.CompilerParams(
            collective_id=0, has_side_effects=True, vmem_limit_bytes=58 * 2**20),
    )(lengths, head_grad, table, hidden, query_weight, key_weight, value_weight)

def attend_kernel(
    dp_count, head_width, queries, upstream, pairs, table_ref, rows_ref,
    squares_out, peer_out,
    rows, grads, mate_grads, rounded, peer_squares,
    rows_load, grad_send, grad_recv, final_send, final_recv, peer_send, peer_recv,
):
    me = lax.axis_index("tensor")
    core = lax.axis_index("dp")
    side = lax.rem(me, 2)
    mate = me + 1 - 2 * side
    blocks, stacked, _ = queries.shape
    step_rows = head_width
    scale = 1.0 / math.sqrt(head_width)
    share = squares_out.shape[1]
    tile = 256
    tiles = share // tile

    barrier = pltpu.get_barrier_semaphore()
    pl.semaphore_signal(barrier, inc=1, device_id={"tensor": mate}, device_id_type=MESH)
    for step in range(1, dp_count):
        peer = lax.rem(core + step, dp_count)
        pl.semaphore_signal(barrier, inc=1, device_id={"dp": peer}, device_id_type=MESH)

    load = pltpu.make_async_copy(rows_ref, rows, rows_load)
    load.start()
    pl.semaphore_wait(barrier, dp_count)

    def grad_copy(block):
        return pltpu.make_async_remote_copy(
            src_ref=grads.at[block], dst_ref=mate_grads.at[block],
            send_sem=grad_send.at[block], recv_sem=grad_recv.at[block],
            device_id={"tensor": mate}, device_id_type=MESH)

    def rows_of(block):
        return slice(block * step_rows, (block + 1) * step_rows)

    def final_copy(block):
        here = rows_of(block)
        return pltpu.make_async_remote_copy(
            src_ref=rounded.at[here], dst_ref=rounded.at[here],
            send_sem=final_send.at[block], recv_sem=final_recv.at[block],
            device_id={"tensor": mate}, device_id_type=MESH)

    def finish(block):
        @pl.when(side == block % 2)
        def _():
            grad_copy(block).wait_recv()
            here = rows_of(block)
            cosine, sine = cosine_sine(table_ref[here, :])
            key_grad = grads[block, :, :head_width] + mate_grads[block, :, :head_width]
            key_grad = key_grad * cosine - swap_halves(key_grad) * sine
            rounded[here, :head_width] = key_grad.astype(jnp.bfloat16)
            rounded[here, head_width:] = (
                grads[block, :, head_width:] + mate_grads[block, :, head_width:]
            ).astype(jnp.bfloat16)
            final_copy(block).start()

    wide = 2 * head_width
    contract_last = (((1,), (1,)), ((), ()))
    for block in reversed(range(blocks)):
        extent = (block + 1) * step_rows
        for chunk in range(stacked // wide):
            chunk_rows = slice(chunk * wide, (chunk + 1) * wide)
            query = queries[block, chunk_rows, :]
            above = upstream[block, chunk_rows, :]
            scores = lax.dot_general(
                pairs[:extent, :head_width], query, contract_last, preferred_element_type=jnp.float32)
            key_at = lax.broadcasted_iota(jnp.int32, (step_rows, wide), 0)
            query_at = lax.rem(lax.broadcasted_iota(jnp.int32, (step_rows, wide), 1), step_rows)
            corner = jnp.where(key_at <= query_at, scores[extent - step_rows:], far_below)
            if block > 0:
                scores = jnp.concatenate([scores[:extent - step_rows], corner], axis=0)
            else:
                scores = corner
            peak = jnp.max(scores, axis=0, keepdims=True)
            powers = jnp.exp2((scores - peak) * (scale * math.log2(math.e)))
            prob = powers * (1.0 / jnp.sum(powers, axis=0, keepdims=True))
            dprob = lax.dot_general(
                pairs[:extent, head_width:], above, contract_last, preferred_element_type=jnp.float32)
            row_dot = jnp.sum(prob * dprob, axis=0, keepdims=True)
            dscore = (prob * (dprob - row_dot) * scale).astype(jnp.bfloat16)
            key_part = jnp.dot(dscore, query, preferred_element_type=jnp.float32)
            value_part = jnp.dot(
                prob.astype(jnp.bfloat16), above, preferred_element_type=jnp.float32)
            key_part = key_part.reshape(block + 1, step_rows, head_width)
            value_part = value_part.reshape(block + 1, step_rows, head_width)
            if block == blocks - 1 and chunk == 0:
                grads[:, :, :head_width] = key_part
                grads[:, :, head_width:] = value_part
            else:
                grads[:block + 1, :, :head_width] += key_part
                grads[:block + 1, :, head_width:] += value_part
        @pl.when(side != block % 2)
        def _():
            grad_copy(block).start()

        if block + 3 < blocks:
            finish(block + 3)

    for block in reversed(range(min(3, blocks))):
        finish(block)
    for block in reversed(range(blocks)):
        @pl.when(side != block % 2)
        def _():
            final_copy(block).wait_recv()

    load.wait()

    def squares_of(start):
        columns = pl.ds(pl.multiple_of(start, tile), tile)
        sample = lax.dot_general(
            rows[:, columns], rounded[...], (((0,), (0,)), ((), ())),
            preferred_element_type=jnp.float32)
        return sample * sample

    def peer_copy(step, index):
        here = pl.ds(pl.multiple_of(index * tile, tile), tile)
        return pltpu.make_async_remote_copy(
            src_ref=peer_squares.at[step - 1, :, here], dst_ref=peer_out.at[step - 1, :, here],
            send_sem=peer_send.at[step - 1, index], recv_sem=peer_recv.at[step - 1, index],
            device_id={"dp": lax.rem(core + step, dp_count)}, device_id_type=MESH)

    for step in range(1, dp_count):
        @pl.loop(0, tiles)
        def _(index):
            here = pl.ds(pl.multiple_of(index * tile, tile), tile)
            start = lax.rem(core + step, dp_count) * share + index * tile
            squares = squares_of(start)
            peer_squares[step - 1, 0, here, :] = squares[:, :head_width]
            peer_squares[step - 1, 1, here, :] = squares[:, head_width:]
            peer_copy(step, index).start()

    @pl.loop(0, tiles)
    def _(index):
        here = pl.ds(pl.multiple_of(index * tile, tile), tile)
        squares = squares_of(core * share + index * tile)
        squares_out[0, here, :] = squares[:, :head_width]
        squares_out[1, here, :] = squares[:, head_width:]

    for block in range(blocks):
        @pl.when(side != block % 2)
        def _():
            grad_copy(block).wait_send()

        @pl.when(side == block % 2)
        def _():
            final_copy(block).wait_send()
    for step in range(1, dp_count):
        @pl.loop(0, tiles)
        def _(index):
            peer_copy(step, index).wait()


def attend(queries, upstream, pairs, table, half_rows, head_width):
    dp_count = lax.axis_size("dp")
    length, half = half_rows.shape
    blocks = length // head_width
    share = half // dp_count
    wide = 2 * head_width
    dma = pltpu.SemaphoreType.DMA
    here = pl.BlockSpec(memory_space=pltpu.VMEM)
    anywhere = pl.BlockSpec(memory_space=pl.ANY)
    return pl.pallas_call(
        functools.partial(attend_kernel, dp_count, head_width),
        out_shape=(
            jax.ShapeDtypeStruct((2, share, head_width), jnp.float32),
            jax.ShapeDtypeStruct((dp_count - 1, 2, share, head_width), jnp.float32),
        ),
        in_specs=[here] * 4 + [anywhere],
        out_specs=(here, anywhere),
        scratch_shapes=[
            pltpu.VMEM((length, half), jnp.bfloat16),
            pltpu.VMEM((blocks, head_width, wide), jnp.float32),
            pltpu.VMEM((blocks, head_width, wide), jnp.float32),
            pltpu.VMEM((length, wide), jnp.bfloat16),
            pltpu.VMEM((dp_count - 1, 2, share, head_width), jnp.float32),
            dma, dma((blocks,)), dma((blocks,)), dma((blocks,)), dma((blocks,)),
            dma((dp_count - 1, share // 256)), dma((dp_count - 1, share // 256)),
        ],
        compiler_params=pltpu.CompilerParams(
            collective_id=1, has_side_effects=True, vmem_limit_bytes=56 * 2**20),
    )(queries, upstream, pairs, table, half_rows)


def local(hidden, query_weight, key_weight, value_weight, head_grad, lengths):
    head_width = key_weight.shape[2]
    length = head_grad.shape[1]
    table = jnp.asarray(turn_table(length, head_width))
    half_rows, queries, pairs, upstream = gather_project(
        lengths, head_grad[0], table, hidden[0], query_weight, key_weight[0], value_weight[0]
    )
    own, peer = attend(
        queries, upstream, pairs.reshape(length, -1), table, half_rows.reshape(length, -1),
        head_width,
    )
    fisher_key = own[:1] + jnp.sum(peer[:, :1], axis=0)
    fisher_value = own[1:] + jnp.sum(peer[:, 1:], axis=0)
    return (fisher_key, fisher_value)


def solution(mesh):
    in_specs = (
        P(("groups", "dp"), "tensor", None),
        P(None, "tensor"),
        P("tensor", None, None),
        P("tensor", None, None),
        P(("groups", "dp"), None, "tensor"),
        P(("groups", "dp")),
    )
    out_specs = (P(("groups", "tensor"), "dp", None), P(("groups", "tensor"), "dp", None))
    return jax.shard_map(local, mesh=mesh, in_specs=in_specs, out_specs=out_specs, check_vma=False)
```
